32 devices in a mesh: section: 4 (over z), tp: 8 (over y, x, core).
Axes of the slice: x: 2, y: 2, z: 4, core: 2. Of those that a mesh axis runs over, the one named last changes fastest.
Arguments:
- hidden_entering: bfloat16 [4, 16, 8192], P('section', None, 'tp'), may hold values from -6 to 6
- layer_norm_gain: bfloat16 [4, 8192], P('section'), may hold values from 0.25 to 1.75
- query_matrix: bfloat16 [4, 8192, 4096], P('section', None, 'tp'), may hold values from -0.0625 to 0.0625
- output_matrix: bfloat16 [4, 4096, 8192], P('section', 'tp'), may hold values from -0.09375 to 0.09375
- adapter_down_weight: bfloat16 [4, 4, 64, 8192], P('section', None, 'tp'), may hold values from -0.0625 to 0.0625
- adapter_up_weight: bfloat16 [4, 4, 64, 4096], P('section', None, None, 'tp'), may hold values from -0.75 to 0.75
- key_value_cache: bfloat16 [4, 3, 16, 32, 1024], P('section', None, 'tp')
- adapter_index: int32 [4, 16], replicated, may hold values from 0 to 3
- cached_lengths: int32 [4, 16], replicated, may hold values from 1 to 32, as said below
Outputs:
- section_out: bfloat16 [4, 3, 16, 8192], P('section', None, None, 'tp')
The draws below stay inside these ranges and needn't reach their ends.
Inputs may be any that keep to these rules, and one draw needn't show every extreme that they name: `cached_lengths`: in every group some request uses all 32 cached positions.
All inputs are finite; a program needn't handle non-finite values.
Results may differ from the reference program's by a relative error of at most 0.03.
Values may be sent and summed in bfloat16 or wider, within the bound.
A program may use at most 64 MiB of HBM per device.

```python
import jax
import jax.numpy as jnp
from jax import lax

MODEL_WIDTH = 8192
HD = 128
HEADS = 32
KVH = 4
ADAPTER_RANK = 64
ADAPTER_COUNT = 4
CTX = 32
TICKS = 3
GROUP_REQUESTS = 16
QUERY_WIDTH = 4096
SECTION_COUNT = 4
N_TP = 8


def draw_cached_lengths(key, part):
    first, second = jax.random.split(jax.random.fold_in(key, 11))
    request_lengths = jax.random.randint(first, (SECTION_COUNT, GROUP_REQUESTS), 1, CTX + 1)
    spot = jax.random.randint(second, (SECTION_COUNT, 1), 0, GROUP_REQUESTS)
    return jnp.where(jnp.arange(GROUP_REQUESTS)[None, :] == spot, CTX, request_lengths).astype(jnp.int32)


def draw_key_value_cache(key, part):
    first = jax.random.fold_in(jax.random.fold_in(key, 23), 0)
    values = jax.random.normal(first, (SECTION_COUNT, TICKS, GROUP_REQUESTS, CTX, 2 * KVH * HD), jnp.float32)
    return values.astype(jnp.bfloat16)


def plant(entries, rng, least, largest):
    index_at = [jax.random.randint(jax.random.fold_in(rng, axis), (), 0, length) for axis, length in enumerate(entries.shape)]
    widest = entries.shape.index(max(entries.shape))
    beside = index_at[:widest] + [(index_at[widest] + 1) % entries.shape[widest]] + index_at[widest + 1:]
    return entries.at[tuple(index_at)].set(least).at[tuple(beside)].set(largest)


def level_of(stream_key, shape, pieces, least, largest):
    level, own = 1.0, jax.random.fold_in(stream_key, 6)
    for dim, shards_of in pieces:
        draws = jnp.exp(jax.random.uniform(jax.random.fold_in(own, dim), (shards_of,), jnp.float32, least / len(pieces), largest / len(pieces)))
        level = level * jnp.repeat(draws, shape[dim] // shards_of).reshape([-1 if axis == dim else 1 for axis in range(len(shape))])
    return level


def bell_draw(stream_key, dims, width, limit, pieces=(), kind=jnp.bfloat16):
    values = jax.random.normal(stream_key, dims, jnp.float32) * width
    if len(pieces) > 0:
        values = level_of(stream_key, dims, pieces, -0.22, 0.18) * values
    return jnp.clip(values, min=-limit, max=limit).astype(kind)


def setup_inputs(seed: int = 0) -> dict:
    streams_of = jax.random.split(jax.random.key(seed), 10)
    hidden_entering = bell_draw(streams_of[0], (SECTION_COUNT, GROUP_REQUESTS, MODEL_WIDTH), 1.0, 6.0, ((0, 4), (2, 8)))
    layer_norm_gain = jnp.clip(1.0 + 0.15 * jax.random.normal(streams_of[1], (SECTION_COUNT, MODEL_WIDTH), jnp.float32), 0.25, 1.75).astype(jnp.bfloat16)
    query_matrix = bell_draw(streams_of[2], (SECTION_COUNT, MODEL_WIDTH, QUERY_WIDTH), MODEL_WIDTH ** -0.5, 0.0625, ((0, 4), (2, 8)))
    output_matrix = bell_draw(streams_of[3], (SECTION_COUNT, QUERY_WIDTH, MODEL_WIDTH), QUERY_WIDTH ** -0.5, 0.09375, ((0, 4), (1, 8)))
    adapter_down_weight = bell_draw(streams_of[4], (SECTION_COUNT, ADAPTER_COUNT, ADAPTER_RANK, MODEL_WIDTH), MODEL_WIDTH ** -0.5, 0.0625, ((0, 4), (2, 8)))
    adapter_up_weight = bell_draw(streams_of[5], (SECTION_COUNT, ADAPTER_COUNT, ADAPTER_RANK, QUERY_WIDTH), ADAPTER_RANK ** -0.5, 0.75, ((0, 4), (3, 8)))
    key_value_cache = draw_key_value_cache(jax.random.fold_in(streams_of[9], 71), 0)
    adapter_index = plant(jax.random.randint(streams_of[7], (SECTION_COUNT, GROUP_REQUESTS), 0, ADAPTER_COUNT), jax.random.fold_in(streams_of[7], 1), 0, ADAPTER_COUNT - 1).astype(jnp.int32)
    cached_lengths = draw_cached_lengths(jax.random.fold_in(streams_of[9], 71), 0)
    return dict(hidden_entering=hidden_entering, layer_norm_gain=layer_norm_gain, query_matrix=query_matrix, output_matrix=output_matrix, adapter_down_weight=adapter_down_weight, adapter_up_weight=adapter_up_weight, key_value_cache=key_value_cache, adapter_index=adapter_index, cached_lengths=cached_lengths)


adapter_scale = 2.0

def layer_index(args):
    x, gain, wq, wo, down_matrix, up_matrix, cache, request_adapters, request_lengths = args
    xf = x.astype(jnp.float32)
    inv = lax.rsqrt(lax.optimization_barrier(jnp.mean(xf * xf, axis=-1, keepdims=True)) + 1e-05)
    xn = (xf * inv * gain.astype(jnp.float32)[None, :]).astype(jnp.bfloat16)
    base_query = jnp.dot(xn, wq, preferred_element_type=jnp.float32)
    onehot = (request_adapters[:, None] == jnp.arange(ADAPTER_COUNT, dtype=jnp.int32)[None, :]).astype(jnp.float32)
    u_all = jnp.dot(xn, down_matrix.reshape(ADAPTER_COUNT * ADAPTER_RANK, MODEL_WIDTH).T, preferred_element_type=jnp.float32)
    u_all = u_all.reshape(GROUP_REQUESTS, ADAPTER_COUNT, ADAPTER_RANK)
    u_sel = lax.optimization_barrier(jnp.sum(u_all * onehot[:, :, None], axis=1)).astype(jnp.bfloat16)
    spread_rows = (onehot.astype(jnp.bfloat16)[:, :, None] * u_sel[:, None, :]).reshape(GROUP_REQUESTS, ADAPTER_COUNT * ADAPTER_RANK)
    adapter_delta = jnp.dot(spread_rows, up_matrix.reshape(ADAPTER_COUNT * ADAPTER_RANK, QUERY_WIDTH), preferred_element_type=jnp.float32)
    query_rows = (base_query + adapter_scale * adapter_delta).astype(jnp.bfloat16)
    group = HEADS // KVH
    qh = query_rows.reshape(GROUP_REQUESTS, KVH, group, HD).astype(jnp.float32)
    keys = cache[:, :, :KVH * HD].reshape(GROUP_REQUESTS, CTX, KVH, HD).astype(jnp.float32)
    values = cache[:, :, KVH * HD:].reshape(GROUP_REQUESTS, CTX, KVH, HD).astype(jnp.float32)
    scores = jnp.einsum('rkgh,rckh->rkgc', qh, keys) * HD ** (-0.5)
    valid = (jnp.arange(CTX, dtype=jnp.int32)[None, :] < request_lengths[:, None])[:, None, None, :]
    scores = jnp.where(valid, scores, -1e+30)
    top = lax.optimization_barrier(jnp.max(scores, axis=-1, keepdims=True))
    expo = jnp.where(valid, jnp.exp(scores - top), 0.0)
    weights = (expo / lax.optimization_barrier(jnp.sum(expo, axis=-1, keepdims=True))).astype(jnp.bfloat16)
    attn = jnp.einsum('rkgc,rckh->rkgh', weights.astype(jnp.float32), values)
    attn = attn.reshape(GROUP_REQUESTS, QUERY_WIDTH).astype(jnp.bfloat16)
    block_list = attn.reshape(GROUP_REQUESTS, N_TP, QUERY_WIDTH // N_TP).astype(jnp.float32)
    weighted_rows = wo.reshape(N_TP, QUERY_WIDTH // N_TP, MODEL_WIDTH).astype(jnp.float32)
    term_list = jnp.einsum('vys,ysj->vyj', block_list, weighted_rows).astype(jnp.bfloat16)
    term_list = lax.optimization_barrier(term_list)
    branch = lax.optimization_barrier(jnp.sum(term_list.astype(jnp.float32), axis=1))
    return (xf + branch).astype(jnp.bfloat16)

def reference(hidden_entering, layer_norm_gain, query_matrix, output_matrix, adapter_down_weight, adapter_up_weight, key_value_cache, adapter_index, cached_lengths):
    hidden_state = hidden_entering
    collected = []
    for step_index in range(TICKS):
        groups = ((jnp.arange(SECTION_COUNT, dtype=jnp.int32) - step_index) % SECTION_COUNT).astype(jnp.int32)
        request_adapters = adapter_index[groups]
        request_lengths = cached_lengths[groups]
        layer_result = lax.map(layer_index, (hidden_state, layer_norm_gain, query_matrix, output_matrix, adapter_down_weight, adapter_up_weight, key_value_cache[:, step_index], request_adapters, request_lengths))
        collected.append(layer_result)
        hidden_state = jnp.roll(layer_result, 1, axis=0)
    return jnp.stack(collected, axis=1)
```

```python
import functools

import jax
import jax.numpy as jnp
from jax import lax
from jax.experimental import pallas as pl
from jax.experimental.pallas import tpu as pltpu
from jax.sharding import PartitionSpec as P

HD = 128
HEADS = 32
KVH = 4
ADAPTER_SCALE = 2.0
LANES = 128
MESH = pl.DeviceIdType.MESH
BF16 = jnp.bfloat16
F32 = jnp.float32


def flipped(me, d):
    value, bit = me, 1
    while bit <= d:
        if d & bit:
            value = value + bit * (1 - 2 * ((me // bit) % 2))
        bit *= 2
    return value


def kernel(
    sections,
    parts,
    adapter_ref,
    lens_ref,
    x_hbm,
    gain_hbm,
    wq_hbm,
    wo_hbm,
    down_hbm,
    up_hbm,
    kv_hbm,
    out_ref,
    wq,
    wo,
    gain,
    up,
    dpair,
    dpair32,
    dchip,
    dparts,
    dcols32,
    dcols,
    kbuf,
    vbuf,
    xbuf,
    ubuf,
    res,
    tbuf,
    sbuf,
    pbuf,
    rbuf,
    wq_sem,
    wo_sem,
    gain_sem,
    up_sem,
    x_sem,
    dp_send,
    dp_recv,
    d_send,
    d_recv,
    kv_send,
    kv_recv,
    x_send,
    x_recv,
    u_send,
    u_recv,
    p_send,
    p_recv,
    r_send,
    r_recv,
    res_send,
    res_recv,
    o_send,
    o_recv,
):
    section = lax.axis_index("section")
    me = lax.axis_index("tp")
    ticks, parts_, rows, share = xbuf.shape
    width = parts * share
    owned, context = kv_hbm.shape[2], kv_hbm.shape[3]
    feats = wq.shape[1]
    heads = feats // HD
    group = HEADS // KVH
    adapters, rank_share = down_hbm.shape[1], down_hbm.shape[2]
    rank_full = up_hbm.shape[2]
    ranks = adapters * rank_share
    full = adapters * rank_full
    nxt = (section + 1) % sections
    prv = (section + sections - 1) % sections
    partner = flipped(me, 1)
    last = ticks - 1

    odd = list(range(parts - 1, 2, -2))
    cross = odd + [1]
    even = [d - 1 for d in odd]
    near_odd = odd[::-1]
    arrival = [0, 1] + near_odd + even[::-1]
    direct = [0] + near_odd

    def cols_of(device):
        return pl.ds(pl.multiple_of(device * share, share), share)

    gain_copy = pltpu.make_async_copy(gain_hbm, gain, gain_sem)
    gain_copy.start()
    x_copy = pltpu.make_async_copy(x_hbm.at[0], xbuf.at[0, 0], x_sem)
    x_copy.start()
    dp_own = []
    for i, d in enumerate(direct):
        copy = pltpu.make_async_copy(
            down_hbm.at[0, :, :, cols_of(flipped(me, d))], dpair.at[0, i], dp_recv.at[0, i]
        )
        copy.start()
        dp_own.append(copy)
    wq_copies = {}
    for d in arrival:
        span = cols_of(flipped(me, d))
        wq_copies[d] = pltpu.make_async_copy(wq_hbm.at[0, span, :], wq.at[span, :], wq_sem.at[d])
        wq_copies[d].start()
    up_copy = pltpu.make_async_copy(up_hbm.at[0], up, up_sem)
    up_copy.start()
    wo_copy = pltpu.make_async_copy(wo_hbm.at[0], wo, wo_sem)
    wo_copy.start()

    barrier = pltpu.get_barrier_semaphore()
    greeted = [(section, flipped(me, d)) for d in range(1, parts)]
    greeted += [(prv, flipped(me, d)) for d in cross] + [(prv, me), (nxt, me)]
    for device in greeted:
        pl.semaphore_signal(barrier, inc=1, device_id=device, device_id_type=MESH)
    pl.semaphore_wait(barrier, len(greeted))

    pending = []

    def send(src, dst, ssem, rsem, device):
        copy = pltpu.make_async_remote_copy(
            src_ref=src,
            dst_ref=dst,
            send_sem=ssem,
            recv_sem=rsem,
            device_id=device,
            device_id_type=MESH,
        )
        copy.start()
        pending.append(copy)
        return copy

    def spread_x(t, src):
        copies = {}
        for d in cross:
            copies[d] = send(
                src, xbuf.at[t, d], x_send.at[t, d], x_recv.at[t, d], (section, flipped(me, d))
            )
        return copies

    def forward_x(t, d):
        return send(
            xbuf.at[t, d],
            xbuf.at[t, d - 1],
            x_send.at[t, d - 1],
            x_recv.at[t, d - 1],
            (section, partner),
        )

    def spread_u(t):
        copies = {}
        for d in range(parts - 1, 0, -1):
            copies[d] = send(
                ubuf.at[t, 0],
                ubuf.at[t, d],
                u_send.at[t, d],
                u_recv.at[t, d],
                (section, flipped(me, d)),
            )
        return copies

    def send_res(t, src):
        return send(src, res.at[t], res_send.at[t], res_recv.at[t], (nxt, me))

    def kv_head(device):
        return (device * heads) // group

    def rows_of(device):
        return pl.ds(pl.multiple_of(device * owned, owned), owned)

    kv_copies = {}

    def send_cache(t):
        for d in cross + [0]:
            peer = flipped(me, d)
            for i, buf in enumerate((kbuf, vbuf)):
                col = pl.multiple_of(i * KVH * HD + kv_head(peer) * HD, HD)
                src = kv_hbm.at[0, t, :, :, pl.ds(col, HD)]
                dst = buf.at[t, rows_of(me)]
                if d == 0:
                    copy = pltpu.make_async_copy(src, dst, kv_recv.at[t, i, 0])
                    copy.start()
                else:
                    copy = send(
                        src, dst, kv_send.at[t, i, d], kv_recv.at[t, i, d], (section, peer)
                    )
                kv_copies[t, i, d] = copy

    def forward_cache(t):
        for d in near_odd:
            for i, buf in enumerate((kbuf, vbuf)):
                kv_copies[t, i, d].wait_recv()
                block = buf.at[t, rows_of(flipped(me, d))]
                kv_copies[t, i, d - 1] = send(
                    block,
                    block,
                    kv_send.at[t, i, d - 1],
                    kv_recv.at[t, i, d - 1],
                    (section, partner),
                )

    def wait_cache(t):
        for i in range(2):
            kv_copies[t, i, 0].wait()
            for d in [1] + even:
                kv_copies[t, i, d].wait_recv()

    d_copies = {}

    def send_down(peers):
        for d in peers:
            peer = flipped(me, d)
            d_copies[d] = send(
                down_hbm.at[0, :, :, cols_of(peer)],
                dparts.at[me],
                d_send.at[d],
                d_recv.at[d],
                (section, peer),
            )

    x_copies = spread_x(0, x_hbm.at[0])
    dp_copies = []
    for i, d in enumerate(direct):
        dp_copies.append(
            send(
                down_hbm.at[0, :, :, cols_of(flipped(partner, d))],
                dpair.at[1, i],
                dp_send.at[i],
                dp_recv.at[1, i],
                (section, partner),
            )
        )
    send_cache(0)
    down_first = [parts - 1, parts - 2]
    down_later = [d for d in range(parts - 1, 0, -1) if d not in down_first]
    send_down(down_first)

    row = lax.broadcasted_iota(jnp.int32, (2 * ranks, LANES), 0)
    col = lax.broadcasted_iota(jnp.int32, (2 * ranks, LANES), 1)
    holder = jnp.where(row < ranks, me, partner)
    spot = row % ranks // rank_share * rank_full + holder * rank_share + row % rank_share
    place = jnp.where(spot % LANES == col, 1.0, 0.0).astype(BF16)

    for i in range(len(direct)):
        dp_own[i].wait()
        for a in range(adapters):
            lo = a * rank_share
            dpair32[i, lo : lo + rank_share, :] = dpair[0, i, a].astype(F32)
    gain_copy.wait()
    x_copy.wait()
    send_res(0, xbuf.at[0, 0])

    for t in range(ticks):
        gidx = (section + sections - t) % sections
        gidx_next = (section + sections - t - 1) % sections

        def adapter_of(index, columns):
            r_id = lax.broadcasted_iota(jnp.int32, (rows, columns), 0)
            chosen = jnp.zeros((rows, columns), jnp.int32)
            for r in range(rows):
                chosen = jnp.where(r_id == r, adapter_ref[index, r], chosen)
            return chosen

        def onehot_of(index):
            a_id = lax.broadcasted_iota(jnp.int32, (rows, full), 1) // rank_full
            return jnp.where(adapter_of(index, full) == a_id, 1.0, 0.0)

        c_id = lax.broadcasted_iota(jnp.int32, (1, rows * context), 1)
        lens = jnp.zeros((1, rows * context), jnp.int32)
        for r in range(rows):
            lens = jnp.where(c_id // context == r, lens_ref[gidx, r], lens)
        if t == 0:
            onehot = onehot_of(gidx)
        else:
            onehot = onehot_next
        m_row = lax.broadcasted_iota(jnp.int32, (heads * rows, rows * context), 0) % rows
        m_col = lax.broadcasted_iota(jnp.int32, (heads * rows, rows * context), 1)
        valid = (m_row == m_col // context) & (m_col % context < lens)

        if t > 0:
            forward_cache(t)

        squares = jnp.zeros((rows, 1), F32)
        acc_u = jnp.zeros((rows, 2 * ranks), F32)
        acc_q = jnp.zeros((rows, feats), F32)
        for d in arrival:
            if d > 0:
                x_copies[d].wait_recv()
            if d in odd:
                x_copies[d - 1] = forward_x(t, d)
            span = cols_of(flipped(me, d))
            xf = xbuf[t, d].astype(F32)
            squares += jnp.sum(xf * xf, axis=-1, keepdims=True)
            h = (xf * gain[:, span].astype(F32)).astype(BF16)
            if t == 0 and d in direct:
                i = direct.index(d)
                dp_copies[i].wait_recv()
                for a in range(adapters):
                    lo = ranks + a * rank_share
                    dpair32[i, lo : lo + rank_share, :] = dpair[1, i, a].astype(F32)
                dchip[i] = dpair32[i].astype(BF16)
                acc_u += lax.dot_general(
                    h, dchip[i], (((1,), (1,)), ((), ())), preferred_element_type=F32
                )
                if d == direct[-1]:
                    a_id = lax.broadcasted_iota(jnp.int32, (rows, 2 * ranks), 1)
                    a_id = a_id // rank_share % adapters
                    picked = jnp.where(adapter_of(gidx, 2 * ranks) == a_id, acc_u, 0.0)
                    ubuf[t, 0] = jnp.dot(
                        picked.astype(BF16), place, preferred_element_type=F32
                    ).astype(BF16)
                    u_copies = spread_u(t)
                    send_down(down_later)
            if t == 0:
                wq_copies[d].wait()
            acc_q += jnp.dot(h, wq[span, :], preferred_element_type=F32)
        inv = lax.rsqrt(squares * (1.0 / width) + 1e-05)
        if t == 0:
            forward_cache(t)
            up_copy.wait()
        u_sum = ubuf[t, 0].astype(F32)
        for d in range(1, parts):
            u_copies[d].wait_recv()
            u_sum += ubuf[t, d].astype(F32)
        u_sum = u_sum * inv
        u_wide = (jnp.concatenate([u_sum] * (full // LANES), axis=1) * onehot).astype(BF16)
        delta = jnp.dot(u_wide, up[...].reshape(full, feats), preferred_element_type=F32)
        query = (acc_q * inv + ADAPTER_SCALE * delta).astype(BF16)

        wait_cache(t)
        qh = jnp.concatenate([query[:, i * HD : (i + 1) * HD] for i in range(heads)], axis=0)
        keys = kbuf[t].reshape(rows * context, HD)
        values = vbuf[t].reshape(rows * context, HD)
        scores = lax.dot_general(
            qh, keys, (((1,), (1,)), ((), ())), preferred_element_type=F32
        ) * HD ** (-0.5)
        scores = jnp.where(valid, scores, -1e30)
        top = jnp.max(scores, axis=-1, keepdims=True)
        expo = jnp.where(valid, jnp.exp(scores - top), 0.0)
        weights = (expo / jnp.sum(expo, axis=-1, keepdims=True)).astype(BF16)
        attn = jnp.dot(weights, values, preferred_element_type=F32).astype(BF16)
        attn = jnp.concatenate([attn[i * rows : (i + 1) * rows] for i in range(heads)], axis=1)

        if t == 0:
            wo_copy.wait()

        def term(d):
            span = cols_of(flipped(me, d))
            return jnp.dot(attn, wo[:, span], preferred_element_type=F32)

        kept = cross if t < last else odd + [0]
        p_copies = {}
        for k in kept:
            e = k - 1 if k % 2 else k + 1
            sbuf[t, e] = term(e).astype(BF16)
            p_copies[k] = send(
                sbuf.at[t, e], pbuf.at[t, k], p_send.at[t, k], p_recv.at[t, k], (section, partner)
            )
        for k in kept:
            tbuf[k] = term(k)
        r_copies = {}
        for k in kept:
            p_copies[k].wait_recv()
            pair = tbuf[k] + pbuf[t, k].astype(F32)
            if k == 0:
                total = pair
                continue
            sbuf[t, k] = pair.astype(BF16)
            target = nxt if t < last else section
            r_copies[k] = send(
                sbuf.at[t, k],
                rbuf.at[t, k],
                r_send.at[t, k],
                r_recv.at[t, k],
                (target, flipped(me, k)),
            )
        if t < last:
            send_cache(t + 1)
        if t == 0:
            own_cols = pltpu.make_async_copy(
                down_hbm.at[0, :, :, cols_of(me)], dparts.at[me], d_recv.at[0]
            )
            own_cols.start()
            own_cols.wait()
            for d in range(1, parts):
                d_copies[d].wait_recv()
            for p in range(parts):
                for a in range(adapters):
                    lo = a * rank_full + p * rank_share
                    dcols32[lo : lo + rank_share, :] = dparts[p, a].astype(F32)
            dcols[...] = dcols32[...].astype(BF16)
        late = [id(copy) for copy in r_copies.values()]
        for copy in pending:
            if id(copy) not in late:
                copy.wait_send()
        pending[:] = list(r_copies.values())
        if t < last:
            onehot_next = onehot_of(gidx_next)
            res_copy = pltpu.make_async_remote_copy(
                src_ref=xbuf.at[t, 0],
                dst_ref=res.at[t],
                send_sem=res_send.at[t],
                recv_sem=res_recv.at[t],
                device_id=(nxt, me),
                device_id_type=MESH,
            )
            res_copy.wait_recv()
            total = res[t].astype(F32)
            for k in cross:
                r_copies[k].wait_recv()
                total += rbuf[t, k].astype(F32)
            result = total.astype(BF16)
            xbuf[t + 1, 0] = result
            x_copies = spread_x(t + 1, xbuf.at[t + 1, 0])
            h = (result.astype(F32) * gain[:, cols_of(me)].astype(F32)).astype(BF16)
            u_part = lax.dot_general(
                h, dcols[...], (((1,), (1,)), ((), ())), preferred_element_type=F32
            )
            u_part = u_part * onehot_next
            u_own = u_part[:, :LANES]
            for i in range(1, full // LANES):
                u_own += u_part[:, i * LANES : (i + 1) * LANES]
            ubuf[t + 1, 0] = u_own.astype(BF16)
            u_copies = spread_u(t + 1)
            if t + 1 < last:
                send_res(t + 1, xbuf.at[t + 1, 0])
            send(
                xbuf.at[t + 1, 0], out_ref.at[0, t], o_send.at[t], o_recv.at[t], (prv, me)
            )
        else:
            for k in near_odd:
                r_copies[k].wait_recv()
                total += rbuf[t, k].astype(F32)
            out_ref[0, t] = (xbuf[t, 0].astype(F32) + total).astype(BF16)

    for t in range(last):
        pltpu.make_async_remote_copy(
            src_ref=xbuf.at[t + 1, 0],
            dst_ref=out_ref.at[0, t],
            send_sem=o_send.at[t],
            recv_sem=o_recv.at[t],
            device_id=(prv, me),
            device_id_type=MESH,
        ).wait_recv()
    for copy in pending:
        copy.wait_send()


def local(
    hidden_entering,
    layer_norm_gain,
    query_matrix,
    output_matrix,
    adapter_down_weight,
    adapter_up_weight,
    key_value_cache,
    adapter_index,
    cached_lengths,
):
    sections = lax.axis_size("section")
    parts = lax.axis_size("tp")
    rows, share = hidden_entering.shape[1:]
    ticks, _, context, _ = key_value_cache.shape[1:]
    width, feats = query_matrix.shape[1:]
    adapters, rank_share = adapter_down_weight.shape[1:3]
    rank_full = adapter_up_weight.shape[2]
    ranks, full = adapters * rank_share, adapters * rank_full
    vmem = pl.BlockSpec(memory_space=pltpu.VMEM)
    smem = pl.BlockSpec(memory_space=pltpu.SMEM)
    hbm = pl.BlockSpec(memory_space=pl.ANY)
    dma = pltpu.SemaphoreType.DMA
    blocks = pltpu.VMEM((ticks, parts, rows, share), BF16)
    return pl.pallas_call(
        functools.partial(kernel, sections, parts),
        out_shape=jax.ShapeDtypeStruct((1, ticks, rows, share), BF16),
        in_specs=[smem, smem] + [hbm] * 7,
        out_specs=vmem,
        scratch_shapes=[
            pltpu.VMEM((width, feats), BF16),
            pltpu.VMEM((feats, width), BF16),
            pltpu.VMEM((1, width), BF16),
            pltpu.VMEM((adapters, rank_full, feats), BF16),
            pltpu.VMEM((2, parts // 2, adapters, rank_share, share), BF16),
            pltpu.VMEM((parts // 2, 2 * ranks, share), F32),
            pltpu.VMEM((parts // 2, 2 * ranks, share), BF16),
            pltpu.VMEM((parts, adapters, rank_share, share), BF16),
            pltpu.VMEM((full, share), F32),
            pltpu.VMEM((full, share), BF16),
            pltpu.VMEM((ticks, rows, context, HD), BF16),
            pltpu.VMEM((ticks, rows, context, HD), BF16),
            blocks,
            pltpu.VMEM((ticks, parts, rows, LANES), BF16),
            pltpu.VMEM((ticks, rows, share), BF16),
            pltpu.VMEM((parts, rows, share), F32),
            blocks,
            blocks,
            blocks,
            dma((parts,)),
            dma(()),
            dma(()),
            dma(()),
            dma(()),
            dma((parts // 2,)),
            dma((2, parts // 2)),
            dma((parts,)),
            dma((parts,)),
            dma((ticks, 2, parts)),
            dma((ticks, 2, parts)),
            dma((ticks, parts)),
            dma((ticks, parts)),
            dma((ticks, parts)),
            dma((ticks, parts)),
            dma((ticks, parts)),
            dma((ticks, parts)),
            dma((ticks, parts)),
            dma((ticks, parts)),
            dma((ticks,)),
            dma((ticks,)),
            dma((ticks,)),
            dma((ticks,)),
        ],
        compiler_params=pltpu.CompilerParams(
            collective_id=0, has_side_effects=True, vmem_limit_bytes=56 << 20
        ),
    )(
        adapter_index,
        cached_lengths,
        hidden_entering,
        layer_norm_gain,
        query_matrix,
        output_matrix,
        adapter_down_weight,
        adapter_up_weight,
        key_value_cache,
    )


def solution(mesh):
    placed = (
        P("section", None, "tp"),
        P("section", None),
        P("section", None, "tp"),
        P("section", "tp", None),
        P("section", None, "tp", None),
        P("section", None, None, "tp"),
        P("section", None, "tp", None, None),
        P(),
        P(),
    )
    return jax.shard_map(
        local, mesh=mesh, in_specs=placed, out_specs=P("section", None, None, "tp"), check_vma=False
    )
```

```python
import functools

import jax
import jax.numpy as jnp
from jax import lax
from jax.experimental import pallas as pl
from jax.experimental.pallas import tpu as pltpu
from jax.sharding import PartitionSpec as P

HD = 128
HEADS = 32
KVH = 4
ADAPTER_SCALE = 2.0
LANES = 128
MESH = pl.DeviceIdType.MESH
BF16 = jnp.bfloat16
F32 = jnp.float32


def flipped(me, d):
    value, bit = me, 1
    while bit <= d:
        if d & bit:
            value = value + bit * (1 - 2 * ((me // bit) % 2))
        bit *= 2
    return value


def kernel(
    sections,
    parts,
    adapter_hbm,
    lens_hbm,
    x_hbm,
    gain_hbm,
    wq_hbm,
    wo_hbm,
    down_hbm,
    up_hbm,
    kv_hbm,
    out_ref,
    adapter_ref,
    lens_ref,
    index_sem,
    wq,
    wo,
    gain,
    up,
    dpair,
    dpair32,
    dchip,
    dparts,
    dcols32,
    dcols,
    kbuf,
    vbuf,
    xbuf,
    ubuf,
    res,
    tbuf,
    sbuf,
    pbuf,
    rbuf,
    wq_sem,
    wo_sem,
    gain_sem,
    up_sem,
    x_sem,
    dp_send,
    dp_recv,
    d_send,
    d_recv,
    kv_send,
    kv_recv,
    x_send,
    x_recv,
    u_send,
    u_recv,
    p_send,
    p_recv,
    r_send,
    r_recv,
    res_send,
    res_recv,
    o_send,
    o_recv,
):
    section = lax.axis_index("section")
    me = lax.axis_index("tp")
    ticks, parts_, rows, share = xbuf.shape
    width = parts * share
    owned, context = kv_hbm.shape[2], kv_hbm.shape[3]
    feats = wq.shape[1]
    heads = feats // HD
    group = HEADS // KVH
    adapters, rank_share = down_hbm.shape[1], down_hbm.shape[2]
    rank_full = up_hbm.shape[2]
    ranks = adapters * rank_share
    full = adapters * rank_full
    nxt = (section + 1) % sections
    prv = (section + sections - 1) % sections
    partner = flipped(me, 1)
    last = ticks - 1

    odd = list(range(parts - 1, 2, -2))
    cross = odd + [1]
    even = [d - 1 for d in odd]
    near_odd = odd[::-1]
    arrival = [0, 1] + near_odd + even[::-1]
    direct = [0] + near_odd

    def cols_of(device):
        return pl.ds(pl.multiple_of(device * share, share), share)

    barrier = pltpu.get_barrier_semaphore()
    greeted = [(section, flipped(me, d)) for d in range(1, parts)]
    greeted += [(prv, flipped(me, d)) for d in cross] + [(prv, me), (nxt, me)]
    for device in greeted:
        pl.semaphore_signal(barrier, inc=1, device_id=device, device_id_type=MESH)

    adapter_copy = pltpu.make_async_copy(adapter_hbm, adapter_ref, index_sem.at[0])
    lens_copy = pltpu.make_async_copy(lens_hbm, lens_ref, index_sem.at[1])
    adapter_copy.start()
    lens_copy.start()
    gain_copy = pltpu.make_async_copy(gain_hbm, gain, gain_sem)
    gain_copy.start()
    x_copy = pltpu.make_async_copy(x_hbm.at[0], xbuf.at[0, 0], x_sem)
    x_copy.start()
    dp_own = []
    for i, d in enumerate(direct):
        copy = pltpu.make_async_copy(
            down_hbm.at[0, :, :, cols_of(flipped(me, d))], dpair.at[0, i], dp_recv.at[0, i]
        )
        copy.start()
        dp_own.append(copy)
    wq_copies = {}
    for d in arrival:
        span = cols_of(flipped(me, d))
        wq_copies[d] = pltpu.make_async_copy(wq_hbm.at[0, span, :], wq.at[span, :], wq_sem.at[d])
        wq_copies[d].start()
    up_copy = pltpu.make_async_copy(up_hbm.at[0], up, up_sem)
    up_copy.start()
    wo_copy = pltpu.make_async_copy(wo_hbm.at[0], wo, wo_sem)
    wo_copy.start()

    pl.semaphore_wait(barrier, len(greeted))

    pending = []

    def send(src, dst, ssem, rsem, device):
        copy = pltpu.make_async_remote_copy(
            src_ref=src,
            dst_ref=dst,
            send_sem=ssem,
            recv_sem=rsem,
            device_id=device,
            device_id_type=MESH,
        )
        copy.start()
        pending.append(copy)
        return copy

    def spread_x(t, src):
        copies = {}
        for d in cross:
            copies[d] = send(
                src, xbuf.at[t, d], x_send.at[t, d], x_recv.at[t, d], (section, flipped(me, d))
            )
        return copies

    def forward_x(t, d):
        return send(
            xbuf.at[t, d],
            xbuf.at[t, d - 1],
            x_send.at[t, d - 1],
            x_recv.at[t, d - 1],
            (section, partner),
        )

    def spread_u(t):
        copies = {}
        for d in range(parts - 1, 0, -1):
            copies[d] = send(
                ubuf.at[t, 0],
                ubuf.at[t, d],
                u_send.at[t, d],
                u_recv.at[t, d],
                (section, flipped(me, d)),
            )
        return copies

    def send_res(t, src):
        return send(src, res.at[t], res_send.at[t], res_recv.at[t], (nxt, me))

    def kv_head(device):
        return (device * heads) // group

    def rows_of(device):
        return pl.ds(pl.multiple_of(device * owned, owned), owned)

    kv_copies = {}

    def send_cache(t):
        for d in cross + [0]:
            peer = flipped(me, d)
            for i, buf in enumerate((kbuf, vbuf)):
                col = pl.multiple_of(i * KVH * HD + kv_head(peer) * HD, HD)
                src = kv_hbm.at[0, t, :, :, pl.ds(col, HD)]
                dst = buf.at[t, rows_of(me)]
                if d == 0:
                    copy = pltpu.make_async_copy(src, dst, kv_recv.at[t, i, 0])
                    copy.start()
                else:
                    copy = send(
                        src, dst, kv_send.at[t, i, d], kv_recv.at[t, i, d], (section, peer)
                    )
                kv_copies[t, i, d] = copy

    def forward_cache(t):
        for d in near_odd:
            for i, buf in enumerate((kbuf, vbuf)):
                kv_copies[t, i, d].wait_recv()
                block = buf.at[t, rows_of(flipped(me, d))]
                kv_copies[t, i, d - 1] = send(
                    block,
                    block,
                    kv_send.at[t, i, d - 1],
                    kv_recv.at[t, i, d - 1],
                    (section, partner),
                )

    def wait_cache(t):
        for i in range(2):
            kv_copies[t, i, 0].wait()
            for d in [1] + even:
                kv_copies[t, i, d].wait_recv()

    d_copies = {}

    def send_down(peers):
        for d in peers:
            peer = flipped(me, d)
            d_copies[d] = send(
                down_hbm.at[0, :, :, cols_of(peer)],
                dparts.at[me],
                d_send.at[d],
                d_recv.at[d],
                (section, peer),
            )

    x_copies = spread_x(0, x_hbm.at[0])
    dp_copies = []
    for i, d in enumerate(direct):
        dp_copies.append(
            send(
                down_hbm.at[0, :, :, cols_of(flipped(partner, d))],
                dpair.at[1, i],
                dp_send.at[i],
                dp_recv.at[1, i],
                (section, partner),
            )
        )
    send_cache(0)

    row = lax.broadcasted_iota(jnp.int32, (2 * ranks, LANES), 0)
    col = lax.broadcasted_iota(jnp.int32, (2 * ranks, LANES), 1)
    holder = jnp.where(row < ranks, me, partner)
    spot = row % ranks // rank_share * rank_full + holder * rank_share + row % rank_share
    place = jnp.where(spot % LANES == col, 1.0, 0.0).astype(BF16)

    for i in range(len(direct)):
        dp_own[i].wait()
        for a in range(adapters):
            lo = a * rank_share
            dpair32[i, lo : lo + rank_share, :] = dpair[0, i, a].astype(F32)
    gain_copy.wait()
    adapter_copy.wait()
    lens_copy.wait()
    x_copy.wait()
    res_copies, out_copies = {}, {}
    if last > 0:
        res_copies[0] = send_res(0, xbuf.at[0, 0])

    for t in range(ticks):
        gidx = (section + sections - t) % sections
        gidx_next = (section + sections - t - 1) % sections

        def adapter_of(index, columns):
            r_id = lax.broadcasted_iota(jnp.int32, (rows, columns), 0)
            chosen = jnp.zeros((rows, columns), jnp.int32)
            for r in range(rows):
                chosen = jnp.where(r_id == r, adapter_ref[index, r], chosen)
            return chosen

        def onehot_of(index):
            a_id = lax.broadcasted_iota(jnp.int32, (rows, full), 1) // rank_full
            return jnp.where(adapter_of(index, full) == a_id, 1.0, 0.0)

        c_id = lax.broadcasted_iota(jnp.int32, (1, rows * context), 1)
        lens = jnp.zeros((1, rows * context), jnp.int32)
        for r in range(rows):
            lens = jnp.where(c_id // context == r, lens_ref[gidx, r], lens)
        if t == 0:
            onehot = onehot_of(gidx)
        else:
            onehot = onehot_next
        m_row = lax.broadcasted_iota(jnp.int32, (heads * rows, rows * context), 0) % rows
        m_col = lax.broadcasted_iota(jnp.int32, (heads * rows, rows * context), 1)
        valid = (m_row == m_col // context) & (m_col % context < lens)

        if t > 0:
            forward_cache(t)

        def scaled(d):
            xf = xbuf[t, d].astype(F32)
            h = (xf * gain[:, cols_of(flipped(me, d))].astype(F32)).astype(BF16)
            return h, jnp.sum(xf * xf, axis=-1, keepdims=True)

        def take(slices):
            for d in slices:
                if d > 0:
                    x_copies[d].wait_recv()
                if d in odd:
                    x_copies[d - 1] = forward_x(t, d)

        def project(slices, acc, squares):
            for d in slices:
                if t == 0:
                    wq_copies[d].wait()
            for d in slices:
                h, square = scaled(d)
                squares += square
                span = cols_of(flipped(me, d))
                acc += jnp.dot(h, wq[span, :], preferred_element_type=F32)
            return acc, squares

        acc_q, squares = jnp.zeros((rows, feats), F32), jnp.zeros((rows, 1), F32)
        far_even = even[0]
        if t == 0:
            acc_u = jnp.zeros((rows, 2 * ranks), F32)
            for i in range(len(direct)):
                dp_copies[i].wait_recv()
                for a in range(adapters):
                    lo = ranks + a * rank_share
                    dpair32[i, lo : lo + rank_share, :] = dpair[1, i, a].astype(F32)
                dchip[i] = dpair32[i].astype(BF16)
            a_id = lax.broadcasted_iota(jnp.int32, (rows, 2 * ranks), 1) // rank_share % adapters
            mine = adapter_of(gidx, 2 * ranks) == a_id
            for slices in ([0] + near_odd[:-1], near_odd[-1:]):
                take(slices)
                for d in slices:
                    acc_u += lax.dot_general(
                        scaled(d)[0],
                        dchip[direct.index(d)],
                        (((1,), (1,)), ((), ())),
                        preferred_element_type=F32,
                    )
            picked = jnp.where(mine, acc_u, 0.0).astype(BF16)
            ubuf[0, 0] = jnp.dot(picked, place, preferred_element_type=F32).astype(BF16)
            u_copies = spread_u(0)
            forward_cache(t)
            send_down(range(parts - 1, 0, -1))
            take([1])
            acc_q, squares = project([0, 1] + near_odd, acc_q, squares)
            take(even)
            acc_q, squares = project(even, acc_q, squares)
            up_copy.wait()
        else:
            for slices in ([0, 1], near_odd[:-1], near_odd[-1:], even[:0:-1]):
                take(slices)
                acc_q, squares = project(slices, acc_q, squares)
        for d in range(1, parts):
            u_copies[d].wait_recv()
        u_sum = ubuf[t, 0].astype(F32)
        for d in range(1, parts):
            u_sum += ubuf[t, d].astype(F32)
        u_wide = (jnp.concatenate([u_sum] * (full // LANES), axis=1) * onehot).astype(BF16)
        delta = jnp.dot(u_wide, up[...].reshape(full, feats), preferred_element_type=F32)
        if t > 0:
            take([far_even])
            acc_q, squares = project([far_even], acc_q, squares)
        inv = lax.rsqrt(squares * (1.0 / width) + 1e-05)
        query = ((acc_q + ADAPTER_SCALE * delta) * inv).astype(BF16)

        wait_cache(t)
        qh = jnp.concatenate([query[:, i * HD : (i + 1) * HD] for i in range(heads)], axis=0)
        keys = kbuf[t].reshape(rows * context, HD)
        values = vbuf[t].reshape(rows * context, HD)
        scores = lax.dot_general(
            qh, keys, (((1,), (1,)), ((), ())), preferred_element_type=F32
        ) * HD ** (-0.5)
        scores = jnp.where(valid, scores, -1e30)
        top = jnp.max(scores, axis=-1, keepdims=True)
        expo = jnp.where(valid, jnp.exp(scores - top), 0.0)
        weights = (expo / jnp.sum(expo, axis=-1, keepdims=True)).astype(BF16)
        attn = jnp.dot(weights, values, preferred_element_type=F32).astype(BF16)
        attn = jnp.concatenate([attn[i * rows : (i + 1) * rows] for i in range(heads)], axis=1)

        if t == 0:
            wo_copy.wait()

        def term(d):
            span = cols_of(flipped(me, d))
            return jnp.dot(attn, wo[:, span], preferred_element_type=F32)

        kept = cross if t < last else odd + [0]
        p_copies = {}
        for ks in (kept[:1], kept[1:]):
            for k in ks:
                e = k - 1 if k % 2 else k + 1
                sbuf[t, e] = term(e).astype(BF16)
            for k in ks:
                e = k - 1 if k % 2 else k + 1
                p_copies[k] = send(
                    sbuf.at[t, e],
                    pbuf.at[t, k],
                    p_send.at[t, k],
                    p_recv.at[t, k],
                    (section, partner),
                )
        for k in kept:
            tbuf[k] = term(k)
        r_copies = {}
        for k in kept:
            p_copies[k].wait_recv()
            pair = tbuf[k] + pbuf[t, k].astype(F32)
            if k == 0:
                total = pair
                continue
            sbuf[t, k] = pair.astype(BF16)
            target = nxt if t < last else section
            r_copies[k] = send(
                sbuf.at[t, k],
                rbuf.at[t, k],
                r_send.at[t, k],
                r_recv.at[t, k],
                (target, flipped(me, k)),
            )
        if t < last:
            send_cache(t + 1)
        if t == 0:
            own_cols = pltpu.make_async_copy(
                down_hbm.at[0, :, :, cols_of(me)], dparts.at[me], d_recv.at[0]
            )
            own_cols.start()
            own_cols.wait()
            for d in range(1, parts):
                d_copies[d].wait_recv()
            for p in range(parts):
                for a in range(adapters):
                    lo = a * rank_full + p * rank_share
                    dcols32[lo : lo + rank_share, :] = dparts[p, a].astype(F32)
            dcols[...] = dcols32[...].astype(BF16)
        late = [id(copy) for copy in r_copies.values()]
        for copy in pending:
            if id(copy) not in late:
                copy.wait_send()
        pending[:] = list(r_copies.values())
        if t < last:
            onehot_next = onehot_of(gidx_next)
            res_copies[t].wait_recv()
            total = res[t].astype(F32)
            for k in cross:
                r_copies[k].wait_recv()
                total += rbuf[t, k].astype(F32)
            result = total.astype(BF16)
            xbuf[t + 1, 0] = result
            x_copies = spread_x(t + 1, xbuf.at[t + 1, 0])
            h = (result.astype(F32) * gain[:, cols_of(me)].astype(F32)).astype(BF16)
            u_part = lax.dot_general(
                h, dcols[...], (((1,), (1,)), ((), ())), preferred_element_type=F32
            )
            u_part = u_part * onehot_next
            u_own = u_part[:, :LANES]
            for i in range(1, full // LANES):
                u_own += u_part[:, i * LANES : (i + 1) * LANES]
            ubuf[t + 1, 0] = u_own.astype(BF16)
            u_copies = spread_u(t + 1)
            if t + 1 < last:
                res_copies[t + 1] = send_res(t + 1, xbuf.at[t + 1, 0])
            out_copies[t] = send(
                xbuf.at[t + 1, 0], out_ref.at[0, t], o_send.at[t], o_recv.at[t], (prv, me)
            )
        else:
            for k in near_odd:
                r_copies[k].wait_recv()
                total += rbuf[t, k].astype(F32)
            out_ref[0, t] = (xbuf[t, 0].astype(F32) + total).astype(BF16)

    for t in range(last):
        out_copies[t].wait_recv()
    for copy in pending:
        copy.wait_send()


def local(
    hidden_entering,
    layer_norm_gain,
    query_matrix,
    output_matrix,
    adapter_down_weight,
    adapter_up_weight,
    key_value_cache,
    adapter_index,
    cached_lengths,
):
    sections = lax.axis_size("section")
    parts = lax.axis_size("tp")
    rows, share = hidden_entering.shape[1:]
    ticks, _, context, _ = key_value_cache.shape[1:]
    width, feats = query_matrix.shape[1:]
    adapters, rank_share = adapter_down_weight.shape[1:3]
    rank_full = adapter_up_weight.shape[2]
    ranks, full = adapters * rank_share, adapters * rank_full
    vmem = pl.BlockSpec(memory_space=pltpu.VMEM)
    hbm = pl.BlockSpec(memory_space=pl.ANY)
    dma = pltpu.SemaphoreType.DMA
    blocks = pltpu.VMEM((ticks, parts, rows, share), BF16)
    return pl.pallas_call(
        functools.partial(kernel, sections, parts),
        out_shape=pltpu.VMEM((1, ticks, rows, share), BF16),
        in_specs=[hbm] * 9,
        out_specs=vmem,
        scratch_shapes=[
            pltpu.SMEM(adapter_index.shape, jnp.int32),
            pltpu.SMEM(cached_lengths.shape, jnp.int32),
            dma((2,)),
            pltpu.VMEM((width, feats), BF16),
            pltpu.VMEM((feats, width), BF16),
            pltpu.VMEM((1, width), BF16),
            pltpu.VMEM((adapters, rank_full, feats), BF16),
            pltpu.VMEM((2, parts // 2, adapters, rank_share, share), BF16),
            pltpu.VMEM((parts // 2, 2 * ranks, share), F32),
            pltpu.VMEM((parts // 2, 2 * ranks, share), BF16),
            pltpu.VMEM((parts, adapters, rank_share, share), BF16),
            pltpu.VMEM((full, share), F32),
            pltpu.VMEM((full, share), BF16),
            pltpu.VMEM((ticks, rows, context, HD), BF16),
            pltpu.VMEM((ticks, rows, context, HD), BF16),
            blocks,
            pltpu.VMEM((ticks, parts, rows, LANES), BF16),
            pltpu.VMEM((ticks, rows, share), BF16),
            pltpu.VMEM((parts, rows, share), F32),
            blocks,
            blocks,
            blocks,
            dma((parts,)),
            dma(()),
            dma(()),
            dma(()),
            dma(()),
            dma((parts // 2,)),
            dma((2, parts // 2)),
            dma((parts,)),
            dma((parts,)),
            dma((ticks, 2, parts)),
            dma((ticks, 2, parts)),
            dma((ticks, parts)),
            dma((ticks, parts)),
            dma((ticks, parts)),
            dma((ticks, parts)),
            dma((ticks, parts)),
            dma((ticks, parts)),
            dma((ticks, parts)),
            dma((ticks, parts)),
            dma((ticks,)),
            dma((ticks,)),
            dma((ticks,)),
            dma((ticks,)),
        ],
        compiler_params=pltpu.CompilerParams(
            collective_id=0, has_side_effects=True, vmem_limit_bytes=56 << 20
        ),
    )(
        adapter_index,
        cached_lengths,
        hidden_entering,
        layer_norm_gain,
        query_matrix,
        output_matrix,
        adapter_down_weight,
        adapter_up_weight,
        key_value_cache,
    )


def solution(mesh):
    placed = (
        P("section", None, "tp"),
        P("section", None),
        P("section", None, "tp"),
        P("section", "tp", None),
        P("section", None, "tp", None),
        P("section", None, None, "tp"),
        P("section", None, "tp", None, None),
        P(),
        P(),
    )
    return jax.shard_map(
        local, mesh=mesh, in_specs=placed, out_specs=P("section", None, None, "tp"), check_vma=False
    )
```

```python
import functools

import jax
import jax.numpy as jnp
from jax import lax
from jax.experimental import pallas as pl
from jax.experimental.pallas import tpu as pltpu
from jax.sharding import PartitionSpec as P

HD = 128
HEADS = 32
KVH = 4
ADAPTER_SCALE = 2.0
LANES = 128
MESH = pl.DeviceIdType.MESH
BF16 = jnp.bfloat16
F32 = jnp.float32


def flipped(me, d):
    value, bit = me, 1
    while bit <= d:
        if d & bit:
            value = value + bit * (1 - 2 * ((me // bit) % 2))
        bit *= 2
    return value


def kernel(
    sections,
    parts,
    adapter_hbm,
    lens_hbm,
    x_hbm,
    gain_hbm,
    wq_hbm,
    wo_hbm,
    down_hbm,
    up_hbm,
    kv_hbm,
    out_ref,
    ready,
    adapter_ref,
    lens_ref,
    index_sem,
    wq,
    wo,
    gain,
    up,
    dpair,
    dpair32,
    dchip,
    dparts,
    dcols32,
    dcols,
    kbuf,
    vbuf,
    xbuf,
    ubuf,
    res,
    tbuf,
    sbuf,
    pbuf,
    rbuf,
    wq_sem,
    wo_sem,
    gain_sem,
    up_sem,
    x_sem,
    dp_send,
    dp_recv,
    d_send,
    d_recv,
    kv_send,
    kv_recv,
    x_send,
    x_recv,
    u_send,
    u_recv,
    p_send,
    p_recv,
    r_send,
    r_recv,
    res_send,
    res_recv,
    o_send,
    o_recv,
):
    section = lax.axis_index("section")
    me = lax.axis_index("tp")
    ticks, parts_, rows, share = xbuf.shape
    width = parts * share
    owned, context = kv_hbm.shape[2], kv_hbm.shape[3]
    feats = wq.shape[1]
    heads = feats // HD
    group = HEADS // KVH
    adapters, rank_share = down_hbm.shape[1], down_hbm.shape[2]
    rank_full = up_hbm.shape[2]
    ranks = adapters * rank_share
    full = adapters * rank_full
    nxt = (section + 1) % sections
    prv = (section + sections - 1) % sections
    partner = flipped(me, 1)
    last = ticks - 1

    odd = list(range(parts - 1, 2, -2))
    cross = odd + [1]
    even = [d - 1 for d in odd]
    near_odd = odd[::-1]
    arrival = [0, 1] + near_odd + even[::-1]
    direct = [0] + near_odd

    def cols_of(device):
        return pl.ds(pl.multiple_of(device * share, share), share)

    barrier = pltpu.get_barrier_semaphore()
    greeted = [(section, flipped(me, d)) for d in range(1, parts)]
    greeted += [(prv, me), (nxt, me)]
    for device in greeted:
        pl.semaphore_signal(barrier, inc=1, device_id=device, device_id_type=MESH)

    adapter_copy = pltpu.make_async_copy(adapter_hbm, adapter_ref, index_sem.at[0])
    lens_copy = pltpu.make_async_copy(lens_hbm, lens_ref, index_sem.at[1])
    adapter_copy.start()
    lens_copy.start()
    gain_copy = pltpu.make_async_copy(gain_hbm, gain, gain_sem)
    gain_copy.start()
    x_copy = pltpu.make_async_copy(x_hbm.at[0], xbuf.at[0, 0], x_sem)
    x_copy.start()
    dp_own = []
    for i, d in enumerate(direct):
        copy = pltpu.make_async_copy(
            down_hbm.at[0, :, :, cols_of(flipped(me, d))], dpair.at[0, i], dp_recv.at[0, i]
        )
        copy.start()
        dp_own.append(copy)
    wq_copies = {}
    for d in arrival:
        span = cols_of(flipped(me, d))
        wq_copies[d] = pltpu.make_async_copy(wq_hbm.at[0, span, :], wq.at[span, :], wq_sem.at[d])
        wq_copies[d].start()
    up_copy = pltpu.make_async_copy(up_hbm.at[0], up, up_sem)
    up_copy.start()
    wo_copy = pltpu.make_async_copy(wo_hbm.at[0], wo, wo_sem)
    wo_copy.start()

    pl.semaphore_wait(barrier, len(greeted))

    pending = []

    def send(src, dst, ssem, rsem, device):
        copy = pltpu.make_async_remote_copy(
            src_ref=src,
            dst_ref=dst,
            send_sem=ssem,
            recv_sem=rsem,
            device_id=device,
            device_id_type=MESH,
        )
        copy.start()
        pending.append(copy)
        return copy

    def spread_x(t, src):
        copies = {}
        for d in cross:
            copies[d] = send(
                src, xbuf.at[t, d], x_send.at[t, d], x_recv.at[t, d], (section, flipped(me, d))
            )
        return copies

    def forward_x(t, d):
        return send(
            xbuf.at[t, d],
            xbuf.at[t, d - 1],
            x_send.at[t, d - 1],
            x_recv.at[t, d - 1],
            (section, partner),
        )

    def spread_u(t):
        copies = {}
        for d in range(parts - 1, 0, -1):
            copies[d] = send(
                ubuf.at[t, 0],
                ubuf.at[t, d],
                u_send.at[t, d],
                u_recv.at[t, d],
                (section, flipped(me, d)),
            )
        return copies

    def send_res(t, src):
        return send(src, res.at[t], res_send.at[t], res_recv.at[t], (nxt, me))

    def kv_head(device):
        return (device * heads) // group

    def rows_of(device):
        return pl.ds(pl.multiple_of(device * owned, owned), owned)

    kv_copies = {}

    def send_cache(t):
        for d in cross + [0]:
            peer = flipped(me, d)
            for i, buf in enumerate((kbuf, vbuf)):
                col = pl.multiple_of(i * KVH * HD + kv_head(peer) * HD, HD)
                src = kv_hbm.at[0, t, :, :, pl.ds(col, HD)]
                dst = buf.at[t, rows_of(me)]
                if d == 0:
                    copy = pltpu.make_async_copy(src, dst, kv_recv.at[t, i, 0])
                    copy.start()
                else:
                    copy = send(
                        src, dst, kv_send.at[t, i, d], kv_recv.at[t, i, d], (section, peer)
                    )
                kv_copies[t, i, d] = copy

    def forward_cache(t):
        for d in near_odd:
            for i, buf in enumerate((kbuf, vbuf)):
                kv_copies[t, i, d].wait_recv()
                block = buf.at[t, rows_of(flipped(me, d))]
                kv_copies[t, i, d - 1] = send(
                    block,
                    block,
                    kv_send.at[t, i, d - 1],
                    kv_recv.at[t, i, d - 1],
                    (section, partner),
                )

    def wait_cache(t):
        for i in range(2):
            kv_copies[t, i, 0].wait()
            for d in [1] + even:
                kv_copies[t, i, d].wait_recv()

    d_copies = {}

    def send_down(peers):
        for d in peers:
            peer = flipped(me, d)
            d_copies[d] = send(
                down_hbm.at[0, :, :, cols_of(peer)],
                dparts.at[me],
                d_send.at[d],
                d_recv.at[d],
                (section, peer),
            )

    x_copies = spread_x(0, x_hbm.at[0])
    pl.semaphore_signal(ready, inc=1, device_id=(prv, me), device_id_type=MESH)
    dp_copies = []
    for i, d in enumerate(direct):
        dp_copies.append(
            send(
                down_hbm.at[0, :, :, cols_of(flipped(partner, d))],
                dpair.at[1, i],
                dp_send.at[i],
                dp_recv.at[1, i],
                (section, partner),
            )
        )
    send_cache(0)

    row = lax.broadcasted_iota(jnp.int32, (2 * ranks, LANES), 0)
    col = lax.broadcasted_iota(jnp.int32, (2 * ranks, LANES), 1)
    holder = jnp.where(row < ranks, me, partner)
    spot = row % ranks // rank_share * rank_full + holder * rank_share + row % rank_share
    place = jnp.where(spot % LANES == col, 1.0, 0.0).astype(BF16)

    for i in range(len(direct)):
        dp_own[i].wait()
        for a in range(adapters):
            lo = a * rank_share
            dpair32[i, lo : lo + rank_share, :] = dpair[0, i, a].astype(F32)
    gain_copy.wait()
    adapter_copy.wait()
    lens_copy.wait()
    x_copy.wait()
    res_copies, out_copies = {}, {}
    if last > 0:
        res_copies[0] = send_res(0, xbuf.at[0, 0])

    for t in range(ticks):
        gidx = (section + sections - t) % sections
        gidx_next = (section + sections - t - 1) % sections

        def adapter_of(index, columns):
            r_id = lax.broadcasted_iota(jnp.int32, (rows, columns), 0)
            chosen = jnp.zeros((rows, columns), jnp.int32)
            for r in range(rows):
                chosen = jnp.where(r_id == r, adapter_ref[index, r], chosen)
            return chosen

        def onehot_of(index):
            a_id = lax.broadcasted_iota(jnp.int32, (rows, full), 1) // rank_full
            return jnp.where(adapter_of(index, full) == a_id, 1.0, 0.0)

        c_id = lax.broadcasted_iota(jnp.int32, (1, rows * context), 1)
        lens = jnp.zeros((1, rows * context), jnp.int32)
        for r in range(rows):
            lens = jnp.where(c_id // context == r, lens_ref[gidx, r], lens)
        if t == 0:
            onehot = onehot_of(gidx)
        else:
            onehot = onehot_next
        m_row = lax.broadcasted_iota(jnp.int32, (heads * rows, rows * context), 0) % rows
        m_col = lax.broadcasted_iota(jnp.int32, (heads * rows, rows * context), 1)
        valid = (m_row == m_col // context) & (m_col % context < lens)

        if t > 0:
            forward_cache(t)

        def scaled(d):
            xf = xbuf[t, d].astype(F32)
            h = (xf * gain[:, cols_of(flipped(me, d))].astype(F32)).astype(BF16)
            return h, jnp.sum(xf * xf, axis=-1, keepdims=True)

        def take(slices):
            for d in slices:
                if d > 0:
                    x_copies[d].wait_recv()
                if d in odd:
                    x_copies[d - 1] = forward_x(t, d)

        def project(slices, acc, squares):
            for d in slices:
                if t == 0:
                    wq_copies[d].wait()
            for d in slices:
                h, square = scaled(d)
                squares += square
                span = cols_of(flipped(me, d))
                acc += jnp.dot(h, wq[span, :], preferred_element_type=F32)
            return acc, squares

        acc_q, squares = jnp.zeros((rows, feats), F32), jnp.zeros((rows, 1), F32)
        far_even = even[0]
        if t == 0:
            acc_u = jnp.zeros((rows, 2 * ranks), F32)
            for i in range(len(direct)):
                dp_copies[i].wait_recv()
                for a in range(adapters):
                    lo = ranks + a * rank_share
                    dpair32[i, lo : lo + rank_share, :] = dpair[1, i, a].astype(F32)
                dchip[i] = dpair32[i].astype(BF16)
            a_id = lax.broadcasted_iota(jnp.int32, (rows, 2 * ranks), 1) // rank_share % adapters
            mine = adapter_of(gidx, 2 * ranks) == a_id
            for slices in ([0] + near_odd[:-1], near_odd[-1:]):
                take(slices)
                for d in slices:
                    acc_u += lax.dot_general(
                        scaled(d)[0],
                        dchip[direct.index(d)],
                        (((1,), (1,)), ((), ())),
                        preferred_element_type=F32,
                    )
            picked = jnp.where(mine, acc_u, 0.0).astype(BF16)
            ubuf[0, 0] = jnp.dot(picked, place, preferred_element_type=F32).astype(BF16)
            u_copies = spread_u(0)
            forward_cache(t)
            send_down(range(parts - 1, 0, -1))
            take([1])
            acc_q, squares = project([0, 1] + near_odd, acc_q, squares)
            take(even)
            acc_q, squares = project(even, acc_q, squares)
            up_copy.wait()
        else:
            for slices in ([0, 1], near_odd[:-1], near_odd[-1:], even[:0:-1]):
                take(slices)
                acc_q, squares = project(slices, acc_q, squares)
        for d in range(1, parts):
            u_copies[d].wait_recv()
        u_sum = ubuf[t, 0].astype(F32)
        for d in range(1, parts):
            u_sum += ubuf[t, d].astype(F32)
        u_wide = (jnp.concatenate([u_sum] * (full // LANES), axis=1) * onehot).astype(BF16)
        delta = jnp.dot(u_wide, up[...].reshape(full, feats), preferred_element_type=F32)
        if t > 0:
            take([far_even])
            acc_q, squares = project([far_even], acc_q, squares)
        inv = lax.rsqrt(squares * (1.0 / width) + 1e-05)
        query = ((acc_q + ADAPTER_SCALE * delta) * inv).astype(BF16)

        wait_cache(t)
        qh = jnp.concatenate([query[:, i * HD : (i + 1) * HD] for i in range(heads)], axis=0)
        keys = kbuf[t].reshape(rows * context, HD)
        values = vbuf[t].reshape(rows * context, HD)
        scores = lax.dot_general(
            qh, keys, (((1,), (1,)), ((), ())), preferred_element_type=F32
        ) * HD ** (-0.5)
        scores = jnp.where(valid, scores, -1e30)
        top = jnp.max(scores, axis=-1, keepdims=True)
        expo = jnp.exp(scores - top)
        scale = 1.0 / jnp.sum(expo, axis=-1, keepdims=True)
        attn = jnp.dot(expo.astype(BF16), values, preferred_element_type=F32)
        attn = (attn * scale).astype(BF16)
        attn = jnp.concatenate([attn[i * rows : (i + 1) * rows] for i in range(heads)], axis=1)

        if t == 0:
            wo_copy.wait()

        def term(d):
            span = cols_of(flipped(me, d))
            return jnp.dot(attn, wo[:, span], preferred_element_type=F32)

        kept = cross if t < last else odd + [0]
        p_copies = {}
        for ks in (kept[:1], kept[1:]):
            for k in ks:
                e = k - 1 if k % 2 else k + 1
                sbuf[t, e] = term(e).astype(BF16)
            for k in ks:
                e = k - 1 if k % 2 else k + 1
                p_copies[k] = send(
                    sbuf.at[t, e],
                    pbuf.at[t, k],
                    p_send.at[t, k],
                    p_recv.at[t, k],
                    (section, partner),
                )
        for k in kept:
            tbuf[k] = term(k)
        if t == 0:
            pl.semaphore_wait(ready, 1)
        r_copies = {}
        for k in kept:
            p_copies[k].wait_recv()
            pair = tbuf[k] + pbuf[t, k].astype(F32)
            if k == 0:
                total = pair
                continue
            sbuf[t, k] = pair.astype(BF16)
            target = nxt if t < last else section
            r_copies[k] = send(
                sbuf.at[t, k],
                rbuf.at[t, k],
                r_send.at[t, k],
                r_recv.at[t, k],
                (target, flipped(me, k)),
            )
        if t < last:
            send_cache(t + 1)
        if t == 0:
            own_cols = pltpu.make_async_copy(
                down_hbm.at[0, :, :, cols_of(me)], dparts.at[me], d_recv.at[0]
            )
            own_cols.start()
            own_cols.wait()
            for d in range(1, parts):
                d_copies[d].wait_recv()
            for p in range(parts):
                for a in range(adapters):
                    lo = a * rank_full + p * rank_share
                    dcols32[lo : lo + rank_share, :] = dparts[p, a].astype(F32)
            dcols[...] = dcols32[...].astype(BF16)
        late = [id(copy) for copy in r_copies.values()]
        for copy in pending:
            if id(copy) not in late:
                copy.wait_send()
        pending[:] = list(r_copies.values())
        if t < last:
            onehot_next = onehot_of(gidx_next)
            res_copies[t].wait_recv()
            total = res[t].astype(F32)
            for k in cross:
                r_copies[k].wait_recv()
                total += rbuf[t, k].astype(F32)
            result = total.astype(BF16)
            xbuf[t + 1, 0] = result
            x_copies = spread_x(t + 1, xbuf.at[t + 1, 0])
            h = (result.astype(F32) * gain[:, cols_of(me)].astype(F32)).astype(BF16)
            u_part = lax.dot_general(
                h, dcols[...], (((1,), (1,)), ((), ())), preferred_element_type=F32
            )
            u_part = u_part * onehot_next
            u_own = u_part[:, :LANES]
            for i in range(1, full // LANES):
                u_own += u_part[:, i * LANES : (i + 1) * LANES]
            ubuf[t + 1, 0] = u_own.astype(BF16)
            u_copies = spread_u(t + 1)
            if t + 1 < last:
                res_copies[t + 1] = send_res(t + 1, xbuf.at[t + 1, 0])
            out_copies[t] = send(
                xbuf.at[t + 1, 0], out_ref.at[0, t], o_send.at[t], o_recv.at[t], (prv, me)
            )
        else:
            for k in near_odd:
                r_copies[k].wait_recv()
                total += rbuf[t, k].astype(F32)
            out_ref[0, t] = (xbuf[t, 0].astype(F32) + total).astype(BF16)

    for t in range(last):
        out_copies[t].wait_recv()
    for copy in pending:
        copy.wait_send()


def local(
    hidden_entering,
    layer_norm_gain,
    query_matrix,
    output_matrix,
    adapter_down_weight,
    adapter_up_weight,
    key_value_cache,
    adapter_index,
    cached_lengths,
):
    sections = lax.axis_size("section")
    parts = lax.axis_size("tp")
    rows, share = hidden_entering.shape[1:]
    ticks, _, context, _ = key_value_cache.shape[1:]
    width, feats = query_matrix.shape[1:]
    adapters, rank_share = adapter_down_weight.shape[1:3]
    rank_full = adapter_up_weight.shape[2]
    ranks, full = adapters * rank_share, adapters * rank_full
    vmem = pl.BlockSpec(memory_space=pltpu.VMEM)
    hbm = pl.BlockSpec(memory_space=pl.ANY)
    dma = pltpu.SemaphoreType.DMA
    blocks = pltpu.VMEM((ticks, parts, rows, share), BF16)
    return pl.pallas_call(
        functools.partial(kernel, sections, parts),
        out_shape=pltpu.VMEM((1, ticks, rows, share), BF16),
        in_specs=[hbm] * 9,
        out_specs=vmem,
        scratch_shapes=[
            pltpu.SemaphoreType.REGULAR,
            pltpu.SMEM(adapter_index.shape, jnp.int32),
            pltpu.SMEM(cached_lengths.shape, jnp.int32),
            dma((2,)),
            pltpu.VMEM((width, feats), BF16),
            pltpu.VMEM((feats, width), BF16),
            pltpu.VMEM((1, width), BF16),
            pltpu.VMEM((adapters, rank_full, feats), BF16),
            pltpu.VMEM((2, parts // 2, adapters, rank_share, share), BF16),
            pltpu.VMEM((parts // 2, 2 * ranks, share), F32),
            pltpu.VMEM((parts // 2, 2 * ranks, share), BF16),
            pltpu.VMEM((parts, adapters, rank_share, share), BF16),
            pltpu.VMEM((full, share), F32),
            pltpu.VMEM((full, share), BF16),
            pltpu.VMEM((ticks, rows, context, HD), BF16),
            pltpu.VMEM((ticks, rows, context, HD), BF16),
            blocks,
            pltpu.VMEM((ticks, parts, rows, LANES), BF16),
            pltpu.VMEM((ticks, rows, share), BF16),
            pltpu.VMEM((parts, rows, share), F32),
            blocks,
            blocks,
            blocks,
            dma((parts,)),
            dma(()),
            dma(()),
            dma(()),
            dma(()),
            dma((parts // 2,)),
            dma((2, parts // 2)),
            dma((parts,)),
            dma((parts,)),
            dma((ticks, 2, parts)),
            dma((ticks, 2, parts)),
            dma((ticks, parts)),
            dma((ticks, parts)),
            dma((ticks, parts)),
            dma((ticks, parts)),
            dma((ticks, parts)),
            dma((ticks, parts)),
            dma((ticks, parts)),
            dma((ticks, parts)),
            dma((ticks,)),
            dma((ticks,)),
            dma((ticks,)),
            dma((ticks,)),
        ],
        compiler_params=pltpu.CompilerParams(
            collective_id=0, has_side_effects=True, vmem_limit_bytes=56 << 20
        ),
    )(
        adapter_index,
        cached_lengths,
        hidden_entering,
        layer_norm_gain,
        query_matrix,
        output_matrix,
        adapter_down_weight,
        adapter_up_weight,
        key_value_cache,
    )


def solution(mesh):
    placed = (
        P("section", None, "tp"),
        P("section", None),
        P("section", None, "tp"),
        P("section", "tp", None),
        P("section", None, "tp", None),
        P("section", None, None, "tp"),
        P("section", None, "tp", None, None),
        P(),
        P(),
    )
    return jax.shard_map(
        local, mesh=mesh, in_specs=placed, out_specs=P("section", None, None, "tp"), check_vma=False
    )
```

```python
import functools

import jax
import jax.numpy as jnp
from jax import lax
from jax.experimental import pallas as pl
from jax.experimental.pallas import tpu as pltpu
from jax.sharding import PartitionSpec as P

HD = 128
HEADS = 32
KVH = 4
ADAPTER_SCALE = 2.0
LANES = 128
MESH = pl.DeviceIdType.MESH
BF16 = jnp.bfloat16
F32 = jnp.float32


def flipped(me, d):
    value, bit = me, 1
    while bit <= d:
        if d & bit:
            value = value + bit * (1 - 2 * ((me // bit) % 2))
        bit *= 2
    return value


def kernel(
    sections,
    parts,
    adapter_hbm,
    lens_hbm,
    x_hbm,
    gain_hbm,
    wq_hbm,
    wo_hbm,
    down_hbm,
    up_hbm,
    kv_hbm,
    out_ref,
    ready,
    adapter_ref,
    lens_ref,
    index_sem,
    wq,
    wo,
    gain,
    up,
    dpair,
    dpair32,
    dchip,
    dparts,
    dcols32,
    dcols,
    kbuf,
    vbuf,
    xbuf,
    ubuf,
    res,
    tbuf,
    sbuf,
    pbuf,
    rbuf,
    wq_sem,
    wo_sem,
    gain_sem,
    up_sem,
    x_sem,
    dp_send,
    dp_recv,
    d_send,
    d_recv,
    kv_send,
    kv_recv,
    x_send,
    x_recv,
    u_send,
    u_recv,
    p_send,
    p_recv,
    r_send,
    r_recv,
    res_send,
    res_recv,
    o_send,
    o_recv,
):
    section = lax.axis_index("section")
    me = lax.axis_index("tp")
    ticks, parts_, rows, share = xbuf.shape
    width = parts * share
    owned, context = kv_hbm.shape[2], kv_hbm.shape[3]
    feats = wq.shape[1]
    heads = feats // HD
    group = HEADS // KVH
    adapters, rank_share = down_hbm.shape[1], down_hbm.shape[2]
    rank_full = up_hbm.shape[2]
    ranks = adapters * rank_share
    full = adapters * rank_full
    nxt = (section + 1) % sections
    prv = (section + sections - 1) % sections
    partner = flipped(me, 1)
    last = ticks - 1

    odd = list(range(parts - 1, 2, -2))
    cross = odd + [1]
    even = [d - 1 for d in odd]
    near_odd = odd[::-1]
    arrival = [0, 1] + near_odd + even[::-1]
    direct = [0] + near_odd

    def cols_of(device):
        return pl.ds(pl.multiple_of(device * share, share), share)

    barrier = pltpu.get_barrier_semaphore()
    greeted = [(section, flipped(me, d)) for d in range(1, parts)]
    greeted += [(prv, me), (nxt, me)]
    for device in greeted:
        pl.semaphore_signal(barrier, inc=1, device_id=device, device_id_type=MESH)

    adapter_copy = pltpu.make_async_copy(adapter_hbm, adapter_ref, index_sem.at[0])
    lens_copy = pltpu.make_async_copy(lens_hbm, lens_ref, index_sem.at[1])
    adapter_copy.start()
    lens_copy.start()
    gain_copy = pltpu.make_async_copy(gain_hbm, gain, gain_sem)
    gain_copy.start()
    x_copy = pltpu.make_async_copy(x_hbm.at[0], xbuf.at[0, 0], x_sem)
    x_copy.start()
    dp_own = []
    for i, d in enumerate(direct):
        copy = pltpu.make_async_copy(
            down_hbm.at[0, :, :, cols_of(flipped(me, d))], dpair.at[0, i], dp_recv.at[0, i]
        )
        copy.start()
        dp_own.append(copy)
    wq_copies = {}
    for d in arrival:
        span = cols_of(flipped(me, d))
        wq_copies[d] = pltpu.make_async_copy(wq_hbm.at[0, span, :], wq.at[span, :], wq_sem.at[d])
        wq_copies[d].start()
    up_copy = pltpu.make_async_copy(up_hbm.at[0], up, up_sem)
    up_copy.start()
    wo_copy = pltpu.make_async_copy(wo_hbm.at[0], wo, wo_sem)
    wo_copy.start()

    pl.semaphore_wait(barrier, len(greeted))

    pending = []

    def send(src, dst, ssem, rsem, device):
        copy = pltpu.make_async_remote_copy(
            src_ref=src,
            dst_ref=dst,
            send_sem=ssem,
            recv_sem=rsem,
            device_id=device,
            device_id_type=MESH,
        )
        copy.start()
        pending.append(copy)
        return copy

    def spread_x(t, src):
        copies = {}
        for d in cross:
            copies[d] = send(
                src, xbuf.at[t, d], x_send.at[t, d], x_recv.at[t, d], (section, flipped(me, d))
            )
        return copies

    def forward_x(t, d):
        return send(
            xbuf.at[t, d],
            xbuf.at[t, d - 1],
            x_send.at[t, d - 1],
            x_recv.at[t, d - 1],
            (section, partner),
        )

    def spread_u(t):
        copies = {}
        for d in range(parts - 1, 0, -1):
            copies[d] = send(
                ubuf.at[t, 0],
                ubuf.at[t, d],
                u_send.at[t, d],
                u_recv.at[t, d],
                (section, flipped(me, d)),
            )
        return copies

    def send_res(t, src):
        return send(src, res.at[t], res_send.at[t], res_recv.at[t], (nxt, me))

    def kv_head(device):
        return (device * heads) // group

    def rows_of(device):
        return pl.ds(pl.multiple_of(device * owned, owned), owned)

    kv_copies = {}

    def send_cache(t):
        for d in cross + [0]:
            peer = flipped(me, d)
            for i, buf in enumerate((kbuf, vbuf)):
                col = pl.multiple_of(i * KVH * HD + kv_head(peer) * HD, HD)
                src = kv_hbm.at[0, t, :, :, pl.ds(col, HD)]
                dst = buf.at[t, rows_of(me)]
                if d == 0:
                    copy = pltpu.make_async_copy(src, dst, kv_recv.at[t, i, 0])
                    copy.start()
                else:
                    copy = send(
                        src, dst, kv_send.at[t, i, d], kv_recv.at[t, i, d], (section, peer)
                    )
                kv_copies[t, i, d] = copy

    def forward_cache(t):
        for d in near_odd:
            for i, buf in enumerate((kbuf, vbuf)):
                kv_copies[t, i, d].wait_recv()
                block = buf.at[t, rows_of(flipped(me, d))]
                kv_copies[t, i, d - 1] = send(
                    block,
                    block,
                    kv_send.at[t, i, d - 1],
                    kv_recv.at[t, i, d - 1],
                    (section, partner),
                )

    def wait_cache(t):
        for i in range(2):
            kv_copies[t, i, 0].wait()
            for d in [1] + even:
                kv_copies[t, i, d].wait_recv()

    d_copies = {}

    def send_down(peers):
        for d in peers:
            peer = flipped(me, d)
            d_copies[d] = send(
                down_hbm.at[0, :, :, cols_of(peer)],
                dparts.at[me],
                d_send.at[d],
                d_recv.at[d],
                (section, peer),
            )

    x_copies = spread_x(0, x_hbm.at[0])
    pl.semaphore_signal(ready, inc=1, device_id=(prv, me), device_id_type=MESH)
    dp_copies = []
    for i, d in enumerate(direct):
        dp_copies.append(
            send(
                down_hbm.at[0, :, :, cols_of(flipped(partner, d))],
                dpair.at[1, i],
                dp_send.at[i],
                dp_recv.at[1, i],
                (section, partner),
            )
        )
    send_cache(0)

    row = lax.broadcasted_iota(jnp.int32, (2 * ranks, LANES), 0)
    col = lax.broadcasted_iota(jnp.int32, (2 * ranks, LANES), 1)
    holder = jnp.where(row < ranks, me, partner)
    spot = row % ranks // rank_share * rank_full + holder * rank_share + row % rank_share
    place = jnp.where(spot % LANES == col, 1.0, 0.0).astype(BF16)

    for i in range(len(direct)):
        dp_own[i].wait()
        for a in range(adapters):
            lo = a * rank_share
            dpair32[i, lo : lo + rank_share, :] = dpair[0, i, a].astype(F32)
    gain_copy.wait()
    adapter_copy.wait()
    lens_copy.wait()
    x_copy.wait()
    res_copies, out_copies = {}, {}
    if last > 0:
        res_copies[0] = send_res(0, xbuf.at[0, 0])

    for t in range(ticks):
        gidx = (section + sections - t) % sections
        gidx_next = (section + sections - t - 1) % sections

        def adapter_of(index, columns):
            r_id = lax.broadcasted_iota(jnp.int32, (rows, columns), 0)
            chosen = jnp.zeros((rows, columns), jnp.int32)
            for r in range(rows):
                chosen = jnp.where(r_id == r, adapter_ref[index, r], chosen)
            return chosen

        def onehot_of(index):
            a_id = lax.broadcasted_iota(jnp.int32, (rows, full), 1) // rank_full
            return jnp.where(adapter_of(index, full) == a_id, 1.0, 0.0)

        c_id = lax.broadcasted_iota(jnp.int32, (1, rows * context), 1)
        lens = jnp.zeros((1, rows * context), jnp.int32)
        for r in range(rows):
            lens = jnp.where(c_id // context == r, lens_ref[gidx, r], lens)
        if t == 0:
            onehot = onehot_of(gidx)
        else:
            onehot = onehot_next
        m_row = lax.broadcasted_iota(jnp.int32, (heads * rows, rows * context), 0) % rows
        m_col = lax.broadcasted_iota(jnp.int32, (heads * rows, rows * context), 1)
        valid = (m_row == m_col // context) & (m_col % context < lens)

        if t > 0:
            forward_cache(t)

        def scaled(d):
            xf = xbuf[t, d].astype(F32)
            h = (xf * gain[:, cols_of(flipped(me, d))].astype(F32)).astype(BF16)
            return h, jnp.sum(xf * xf, axis=-1, keepdims=True)

        def take(slices):
            for d in slices:
                if d > 0:
                    x_copies[d].wait_recv()
                if d in odd:
                    x_copies[d - 1] = forward_x(t, d)

        def project(slices, acc, squares):
            for d in slices:
                if t == 0:
                    wq_copies[d].wait()
            for d in slices:
                h, square = scaled(d)
                squares += square
                span = cols_of(flipped(me, d))
                acc += jnp.dot(h, wq[span, :], preferred_element_type=F32)
            return acc, squares

        acc_q, squares = jnp.zeros((rows, feats), F32), jnp.zeros((rows, 1), F32)
        far_even = even[0]
        if t == 0:
            acc_u = jnp.zeros((rows, 2 * ranks), F32)
            for i in range(len(direct)):
                dp_copies[i].wait_recv()
                for a in range(adapters):
                    lo = ranks + a * rank_share
                    dpair32[i, lo : lo + rank_share, :] = dpair[1, i, a].astype(F32)
                dchip[i] = dpair32[i].T.astype(BF16)
            a_id = lax.broadcasted_iota(jnp.int32, (rows, 2 * ranks), 1) // rank_share % adapters
            mine = adapter_of(gidx, 2 * ranks) == a_id
            for slices in ([0] + near_odd[:-1], near_odd[-1:]):
                take(slices)
                for d in slices:
                    acc_u += jnp.dot(
                        scaled(d)[0], dchip[direct.index(d)], preferred_element_type=F32
                    )
            picked = jnp.where(mine, acc_u, 0.0).astype(BF16)
            ubuf[0, 0] = jnp.dot(picked, place, preferred_element_type=F32).astype(BF16)
            u_copies = spread_u(0)
            forward_cache(t)
            send_down(range(parts - 1, 0, -1))
            take([1])
            acc_q, squares = project([0, 1] + near_odd, acc_q, squares)
            take(even)
            acc_q, squares = project(even, acc_q, squares)
            up_copy.wait()
        else:
            for slices in ([0, 1], near_odd, even[:0:-1]):
                take(slices)
                acc_q, squares = project(slices, acc_q, squares)
        for d in range(1, parts):
            u_copies[d].wait_recv()
        u_sum = ubuf[t, 0].astype(F32)
        for d in range(1, parts):
            u_sum += ubuf[t, d].astype(F32)
        u_wide = (jnp.concatenate([u_sum] * (full // LANES), axis=1) * onehot).astype(BF16)
        delta = jnp.dot(u_wide, up[...].reshape(full, feats), preferred_element_type=F32)
        if t > 0:
            take([far_even])
            acc_q, squares = project([far_even], acc_q, squares)
        inv = lax.rsqrt(squares * (1.0 / width) + 1e-05)
        query = ((acc_q + ADAPTER_SCALE * delta) * inv).astype(BF16)

        wait_cache(t)
        qh = jnp.concatenate([query[:, i * HD : (i + 1) * HD] for i in range(heads)], axis=0)
        keys = kbuf[t].reshape(rows * context, HD)
        values = vbuf[t].reshape(rows * context, HD)
        scores = lax.dot_general(
            qh, keys, (((1,), (1,)), ((), ())), preferred_element_type=F32
        ) * HD ** (-0.5)
        scores = jnp.where(valid, scores, -1e30)
        top = jnp.max(scores, axis=-1, keepdims=True)
        expo = jnp.exp(scores - top)
        scale = 1.0 / jnp.sum(expo, axis=-1, keepdims=True)
        attn = jnp.dot(expo.astype(BF16), values, preferred_element_type=F32)
        attn = (attn * scale).astype(BF16)
        attn = jnp.concatenate([attn[i * rows : (i + 1) * rows] for i in range(heads)], axis=1)

        if t == 0:
            wo_copy.wait()

        def term(d):
            span = cols_of(flipped(me, d))
            return jnp.dot(attn, wo[:, span], preferred_element_type=F32)

        kept = cross if t < last else odd + [0]
        p_copies = {}
        for ks in (kept[:1], kept[1:]):
            for k in ks:
                e = k - 1 if k % 2 else k + 1
                sbuf[t, e] = term(e).astype(BF16)
            for k in ks:
                e = k - 1 if k % 2 else k + 1
                p_copies[k] = send(
                    sbuf.at[t, e],
                    pbuf.at[t, k],
                    p_send.at[t, k],
                    p_recv.at[t, k],
                    (section, partner),
                )
        if t == 0:
            pl.semaphore_wait(ready, 1)
        r_copies = {}
        for k in kept:
            if k == kept[0]:
                own_terms = {j: term(j) for j in kept[:2]}
            if k == kept[1]:
                own_terms.update({j: term(j) for j in kept[2:]})
            p_copies[k].wait_recv()
            pair = own_terms[k] + pbuf[t, k].astype(F32)
            if k == 0:
                total = pair
                continue
            sbuf[t, k] = pair.astype(BF16)
            target = nxt if t < last else section
            r_copies[k] = send(
                sbuf.at[t, k],
                rbuf.at[t, k],
                r_send.at[t, k],
                r_recv.at[t, k],
                (target, flipped(me, k)),
            )
        if t < last:
            send_cache(t + 1)
        if t == 0:
            own_cols = pltpu.make_async_copy(
                down_hbm.at[0, :, :, cols_of(me)], dparts.at[me], d_recv.at[0]
            )
            own_cols.start()
            own_cols.wait()
            for d in range(1, parts):
                d_copies[d].wait_recv()
            for p in range(parts):
                for a in range(adapters):
                    lo = a * rank_full + p * rank_share
                    dcols32[lo : lo + rank_share, :] = dparts[p, a].astype(F32)
            dcols[...] = dcols32[...].T.astype(BF16)
        late = [id(copy) for copy in r_copies.values()]
        for copy in pending:
            if id(copy) not in late:
                copy.wait_send()
        pending[:] = list(r_copies.values())
        if t < last:
            onehot_next = onehot_of(gidx_next)
            res_copies[t].wait_recv()
            total = res[t].astype(F32)
            for k in cross:
                r_copies[k].wait_recv()
                total += rbuf[t, k].astype(F32)
            result = total.astype(BF16)
            xbuf[t + 1, 0] = result
            x_copies = spread_x(t + 1, xbuf.at[t + 1, 0])
            h = (result.astype(F32) * gain[:, cols_of(me)].astype(F32)).astype(BF16)
            u_part = jnp.dot(h, dcols[...], preferred_element_type=F32)
            u_part = u_part * onehot_next
            u_own = u_part[:, :LANES]
            for i in range(1, full // LANES):
                u_own += u_part[:, i * LANES : (i + 1) * LANES]
            ubuf[t + 1, 0] = u_own.astype(BF16)
            u_copies = spread_u(t + 1)
            if t + 1 < last:
                res_copies[t + 1] = send_res(t + 1, xbuf.at[t + 1, 0])
            out_copies[t] = send(
                xbuf.at[t + 1, 0], out_ref.at[0, t], o_send.at[t], o_recv.at[t], (prv, me)
            )
        else:
            for k in near_odd:
                r_copies[k].wait_recv()
                total += rbuf[t, k].astype(F32)
            out_ref[0, t] = (xbuf[t, 0].astype(F32) + total).astype(BF16)

    for t in range(last):
        out_copies[t].wait_recv()
    for copy in pending:
        copy.wait_send()


def local(
    hidden_entering,
    layer_norm_gain,
    query_matrix,
    output_matrix,
    adapter_down_weight,
    adapter_up_weight,
    key_value_cache,
    adapter_index,
    cached_lengths,
):
    sections = lax.axis_size("section")
    parts = lax.axis_size("tp")
    rows, share = hidden_entering.shape[1:]
    ticks, _, context, _ = key_value_cache.shape[1:]
    width, feats = query_matrix.shape[1:]
    adapters, rank_share = adapter_down_weight.shape[1:3]
    rank_full = adapter_up_weight.shape[2]
    ranks, full = adapters * rank_share, adapters * rank_full
    vmem = pl.BlockSpec(memory_space=pltpu.VMEM)
    hbm = pl.BlockSpec(memory_space=pl.ANY)
    dma = pltpu.SemaphoreType.DMA
    blocks = pltpu.VMEM((ticks, parts, rows, share), BF16)
    return pl.pallas_call(
        functools.partial(kernel, sections, parts),
        out_shape=pltpu.VMEM((1, ticks, rows, share), BF16),
        in_specs=[hbm] * 9,
        out_specs=vmem,
        scratch_shapes=[
            pltpu.SemaphoreType.REGULAR,
            pltpu.SMEM(adapter_index.shape, jnp.int32),
            pltpu.SMEM(cached_lengths.shape, jnp.int32),
            dma((2,)),
            pltpu.VMEM((width, feats), BF16),
            pltpu.VMEM((feats, width), BF16),
            pltpu.VMEM((1, width), BF16),
            pltpu.VMEM((adapters, rank_full, feats), BF16),
            pltpu.VMEM((2, parts // 2, adapters, rank_share, share), BF16),
            pltpu.VMEM((parts // 2, 2 * ranks, share), F32),
            pltpu.VMEM((parts // 2, share, 2 * ranks), BF16),
            pltpu.VMEM((parts, adapters, rank_share, share), BF16),
            pltpu.VMEM((full, share), F32),
            pltpu.VMEM((share, full), BF16),
            pltpu.VMEM((ticks, rows, context, HD), BF16),
            pltpu.VMEM((ticks, rows, context, HD), BF16),
            blocks,
            pltpu.VMEM((ticks, parts, rows, LANES), BF16),
            pltpu.VMEM((ticks, rows, share), BF16),
            pltpu.VMEM((parts, rows, share), F32),
            blocks,
            blocks,
            blocks,
            dma((parts,)),
            dma(()),
            dma(()),
            dma(()),
            dma(()),
            dma((parts // 2,)),
            dma((2, parts // 2)),
            dma((parts,)),
            dma((parts,)),
            dma((ticks, 2, parts)),
            dma((ticks, 2, parts)),
            dma((ticks, parts)),
            dma((ticks, parts)),
            dma((ticks, parts)),
            dma((ticks, parts)),
            dma((ticks, parts)),
            dma((ticks, parts)),
            dma((ticks, parts)),
            dma((ticks, parts)),
            dma((ticks,)),
            dma((ticks,)),
            dma((ticks,)),
            dma((ticks,)),
        ],
        compiler_params=pltpu.CompilerParams(
            collective_id=0, has_side_effects=True, vmem_limit_bytes=56 << 20
        ),
    )(
        adapter_index,
        cached_lengths,
        hidden_entering,
        layer_norm_gain,
        query_matrix,
        output_matrix,
        adapter_down_weight,
        adapter_up_weight,
        key_value_cache,
    )


def solution(mesh):
    placed = (
        P("section", None, "tp"),
        P("section", None),
        P("section", None, "tp"),
        P("section", "tp", None),
        P("section", None, "tp", None),
        P("section", None, None, "tp"),
        P("section", None, "tp", None, None),
        P(),
        P(),
    )
    return jax.shard_map(
        local, mesh=mesh, in_specs=placed, out_specs=P("section", None, None, "tp"), check_vma=False
    )
```

```python
import functools

import jax
import jax.numpy as jnp
from jax import lax
from jax.experimental import pallas as pl
from jax.experimental.pallas import tpu as pltpu
from jax.sharding import PartitionSpec as P

HD = 128
HEADS = 32
KVH = 4
ADAPTER_SCALE = 2.0
LANES = 128
MESH = pl.DeviceIdType.MESH
BF16 = jnp.bfloat16
F32 = jnp.float32


def flipped(me, d):
    value, bit = me, 1
    while bit <= d:
        if d & bit:
            value = value + bit * (1 - 2 * ((me // bit) % 2))
        bit *= 2
    return value


def kernel(
    sections,
    parts,
    adapter_hbm,
    lens_hbm,
    x_hbm,
    gain_hbm,
    wq_hbm,
    wo_hbm,
    down_hbm,
    up_hbm,
    kv_hbm,
    out_ref,
    ready,
    adapter_ref,
    lens_ref,
    index_sem,
    wq,
    wo,
    gain,
    up,
    dpair,
    dpair32,
    dchip,
    dparts,
    dcols32,
    dcols,
    kbuf,
    vbuf,
    xbuf,
    ubuf,
    res,
    tbuf,
    sbuf,
    pbuf,
    rbuf,
    wq_sem,
    wo_sem,
    gain_sem,
    up_sem,
    x_sem,
    dp_send,
    dp_recv,
    d_send,
    d_recv,
    kv_send,
    kv_recv,
    x_send,
    x_recv,
    u_send,
    u_recv,
    p_send,
    p_recv,
    r_send,
    r_recv,
    res_send,
    res_recv,
    o_send,
    o_recv,
):
    section = lax.axis_index("section")
    me = lax.axis_index("tp")
    ticks, parts_, rows, share = xbuf.shape
    width = parts * share
    owned, context = kv_hbm.shape[2], kv_hbm.shape[3]
    feats = wq.shape[1]
    heads = feats // HD
    group = HEADS // KVH
    adapters, rank_share = down_hbm.shape[1], down_hbm.shape[2]
    rank_full = up_hbm.shape[2]
    ranks = adapters * rank_share
    full = adapters * rank_full
    nxt = (section + 1) % sections
    prv = (section + sections - 1) % sections
    partner = flipped(me, 1)
    last = ticks - 1

    odd = list(range(parts - 1, 2, -2))
    cross = odd + [1]
    even = [d - 1 for d in odd]
    near_odd = odd[::-1]
    arrival = [0, 1] + near_odd + even[::-1]
    direct = [0] + near_odd

    def cols_of(device):
        return pl.ds(pl.multiple_of(device * share, share), share)

    barrier = pltpu.get_barrier_semaphore()
    greeted = [(section, flipped(me, d)) for d in range(1, parts)]
    greeted += [(prv, me), (nxt, me)]
    for device in greeted:
        pl.semaphore_signal(barrier, inc=1, device_id=device, device_id_type=MESH)

    adapter_copy = pltpu.make_async_copy(adapter_hbm, adapter_ref, index_sem.at[0])
    lens_copy = pltpu.make_async_copy(lens_hbm, lens_ref, index_sem.at[1])
    adapter_copy.start()
    lens_copy.start()
    gain_copy = pltpu.make_async_copy(gain_hbm, gain, gain_sem)
    gain_copy.start()
    x_copy = pltpu.make_async_copy(x_hbm.at[0], xbuf.at[0, 0], x_sem)
    x_copy.start()
    dp_own = []
    for i, d in enumerate(direct):
        copy = pltpu.make_async_copy(
            down_hbm.at[0, :, :, cols_of(flipped(me, d))], dpair.at[0, i], dp_recv.at[0, i]
        )
        copy.start()
        dp_own.append(copy)
    wq_copies = {}
    for d in arrival:
        span = cols_of(flipped(me, d))
        wq_copies[d] = pltpu.make_async_copy(wq_hbm.at[0, span, :], wq.at[span, :], wq_sem.at[d])
        wq_copies[d].start()
    up_copy = pltpu.make_async_copy(up_hbm.at[0], up, up_sem)
    up_copy.start()
    wo_copy = pltpu.make_async_copy(wo_hbm.at[0], wo, wo_sem)
    wo_copy.start()

    pl.semaphore_wait(barrier, len(greeted))

    pending = []

    def send(src, dst, ssem, rsem, device):
        copy = pltpu.make_async_remote_copy(
            src_ref=src,
            dst_ref=dst,
            send_sem=ssem,
            recv_sem=rsem,
            device_id=device,
            device_id_type=MESH,
        )
        copy.start()
        pending.append(copy)
        return copy

    def spread_x(t, src):
        copies = {}
        for d in cross:
            copies[d] = send(
                src, xbuf.at[t, d], x_send.at[t, d], x_recv.at[t, d], (section, flipped(me, d))
            )
        return copies

    def forward_x(t, d):
        return send(
            xbuf.at[t, d],
            xbuf.at[t, d - 1],
            x_send.at[t, d - 1],
            x_recv.at[t, d - 1],
            (section, partner),
        )

    def spread_u(t):
        copies = {}
        for d in range(parts - 1, 0, -1):
            copies[d] = send(
                ubuf.at[t, 0],
                ubuf.at[t, d],
                u_send.at[t, d],
                u_recv.at[t, d],
                (section, flipped(me, d)),
            )
        return copies

    def send_res(t, src):
        return send(src, res.at[t], res_send.at[t], res_recv.at[t], (nxt, me))

    def kv_head(device):
        return (device * heads) // group

    def rows_of(device):
        return pl.ds(pl.multiple_of(device * owned, owned), owned)

    kv_copies = {}

    def send_cache(t):
        for d in cross + [0]:
            peer = flipped(me, d)
            for i, buf in enumerate((kbuf, vbuf)):
                col = pl.multiple_of(i * KVH * HD + kv_head(peer) * HD, HD)
                src = kv_hbm.at[0, t, :, :, pl.ds(col, HD)]
                dst = buf.at[t, rows_of(me)]
                if d == 0:
                    copy = pltpu.make_async_copy(src, dst, kv_recv.at[t, i, 0])
                    copy.start()
                else:
                    copy = send(
                        src, dst, kv_send.at[t, i, d], kv_recv.at[t, i, d], (section, peer)
                    )
                kv_copies[t, i, d] = copy

    def forward_cache(t):
        for d in near_odd:
            for i, buf in enumerate((kbuf, vbuf)):
                kv_copies[t, i, d].wait_recv()
                block = buf.at[t, rows_of(flipped(me, d))]
                kv_copies[t, i, d - 1] = send(
                    block,
                    block,
                    kv_send.at[t, i, d - 1],
                    kv_recv.at[t, i, d - 1],
                    (section, partner),
                )

    def wait_cache(t):
        for i in range(2):
            kv_copies[t, i, 0].wait()
            for d in [1] + even:
                kv_copies[t, i, d].wait_recv()

    d_copies = {}

    def send_down(peers):
        for d in peers:
            peer = flipped(me, d)
            d_copies[d] = send(
                down_hbm.at[0, :, :, cols_of(peer)],
                dparts.at[me],
                d_send.at[d],
                d_recv.at[d],
                (section, peer),
            )

    x_copies = spread_x(0, x_hbm.at[0])
    pl.semaphore_signal(ready, inc=1, device_id=(prv, me), device_id_type=MESH)
    dp_copies = []
    for i, d in enumerate(direct):
        dp_copies.append(
            send(
                down_hbm.at[0, :, :, cols_of(flipped(partner, d))],
                dpair.at[1, i],
                dp_send.at[i],
                dp_recv.at[1, i],
                (section, partner),
            )
        )
    send_cache(0)

    row = lax.broadcasted_iota(jnp.int32, (2 * ranks, LANES), 0)
    col = lax.broadcasted_iota(jnp.int32, (2 * ranks, LANES), 1)
    holder = jnp.where(row < ranks, me, partner)
    spot = row % ranks // rank_share * rank_full + holder * rank_share + row % rank_share
    place = jnp.where(spot % LANES == col, 1.0, 0.0).astype(BF16)

    for i in range(len(direct)):
        dp_own[i].wait()
        for a in range(adapters):
            lo = a * rank_share
            dpair32[i, lo : lo + rank_share, :] = dpair[0, i, a].astype(F32)
    gain_copy.wait()
    adapter_copy.wait()
    lens_copy.wait()
    x_copy.wait()
    res_copies, out_copies = {}, {}
    if last > 0:
        res_copies[0] = send_res(0, xbuf.at[0, 0])

    for t in range(ticks):
        gidx = (section + sections - t) % sections
        gidx_next = (section + sections - t - 1) % sections

        def adapter_of(index, columns):
            r_id = lax.broadcasted_iota(jnp.int32, (rows, columns), 0)
            chosen = jnp.zeros((rows, columns), jnp.int32)
            for r in range(rows):
                chosen = jnp.where(r_id == r, adapter_ref[index, r], chosen)
            return chosen

        def onehot_of(index):
            a_id = lax.broadcasted_iota(jnp.int32, (rows, full), 1) // rank_full
            return jnp.where(adapter_of(index, full) == a_id, 1.0, 0.0)

        c_id = lax.broadcasted_iota(jnp.int32, (1, rows * context), 1)
        lens = jnp.zeros((1, rows * context), jnp.int32)
        for r in range(rows):
            lens = jnp.where(c_id // context == r, lens_ref[gidx, r], lens)
        if t == 0:
            onehot = onehot_of(gidx)
        else:
            onehot = onehot_next
        m_row = lax.broadcasted_iota(jnp.int32, (heads * rows, rows * context), 0) % rows
        m_col = lax.broadcasted_iota(jnp.int32, (heads * rows, rows * context), 1)
        valid = (m_row == m_col // context) & (m_col % context < lens)

        if t > 0:
            forward_cache(t)

        def scaled(d):
            xf = xbuf[t, d].astype(F32)
            h = (xf * gain[:, cols_of(flipped(me, d))].astype(F32)).astype(BF16)
            return h, jnp.sum(xf * xf, axis=-1, keepdims=True)

        def take(slices):
            for d in slices:
                if d > 0:
                    x_copies[d].wait_recv()
                if d in odd:
                    x_copies[d - 1] = forward_x(t, d)

        def project(slices, acc, squares):
            for d in slices:
                if t == 0:
                    wq_copies[d].wait()
            for d in slices:
                h, square = scaled(d)
                squares += square
                span = cols_of(flipped(me, d))
                acc += jnp.dot(h, wq[span, :], preferred_element_type=F32)
            return acc, squares

        acc_q, squares = jnp.zeros((rows, feats), F32), jnp.zeros((rows, 1), F32)
        far_even = even[0]
        if t == 0:
            acc_u = jnp.zeros((rows, 2 * ranks), F32)
            for i in range(len(direct)):
                dp_copies[i].wait_recv()
                for a in range(adapters):
                    lo = ranks + a * rank_share
                    dpair32[i, lo : lo + rank_share, :] = dpair[1, i, a].astype(F32)
                dchip[i] = dpair32[i].T.astype(BF16)
            a_id = lax.broadcasted_iota(jnp.int32, (rows, 2 * ranks), 1) // rank_share % adapters
            mine = adapter_of(gidx, 2 * ranks) == a_id
            for slices in ([0] + near_odd[:-1], near_odd[-1:]):
                take(slices)
                for d in slices:
                    acc_u += jnp.dot(
                        scaled(d)[0], dchip[direct.index(d)], preferred_element_type=F32
                    )
            picked = jnp.where(mine, acc_u, 0.0).astype(BF16)
            ubuf[0, 0] = jnp.dot(picked, place, preferred_element_type=F32).astype(BF16)
            u_copies = spread_u(0)
            forward_cache(t)
            send_down(range(parts - 1, 0, -1))
            take([1])
            acc_q, squares = project([0, 1] + near_odd, acc_q, squares)
            take(even)
            acc_q, squares = project(even, acc_q, squares)
            up_copy.wait()
        else:
            for slices in ([0, 1], near_odd, even[:0:-1]):
                take(slices)
                acc_q, squares = project(slices, acc_q, squares)
                if slices[0] == 0:
                    wait_cache(t)
                    keys = kbuf[t].reshape(rows * context, HD).astype(F32).T.astype(BF16)
        for d in range(1, parts):
            u_copies[d].wait_recv()
        u_sum = ubuf[t, 0].astype(F32)
        for d in range(1, parts):
            u_sum += ubuf[t, d].astype(F32)
        u_wide = (jnp.concatenate([u_sum] * (full // LANES), axis=1) * onehot).astype(BF16)
        delta = jnp.dot(u_wide, up[...].reshape(full, feats), preferred_element_type=F32)
        if t > 0:
            take([far_even])
            acc_q, squares = project([far_even], acc_q, squares)
        inv = lax.rsqrt(squares * (1.0 / width) + 1e-05)
        query = ((acc_q + ADAPTER_SCALE * delta) * inv).astype(BF16)

        if t == 0:
            wait_cache(t)
            keys = kbuf[t].reshape(rows * context, HD).astype(F32).T.astype(BF16)
        qh = jnp.concatenate([query[:, i * HD : (i + 1) * HD] for i in range(heads)], axis=0)
        values = vbuf[t].reshape(rows * context, HD)
        scores = jnp.dot(qh, keys, preferred_element_type=F32) * HD ** (-0.5)
        scores = jnp.where(valid, scores, -1e30)
        top = jnp.max(scores, axis=-1, keepdims=True)
        expo = jnp.exp(scores - top)
        scale = 1.0 / jnp.sum(expo, axis=-1, keepdims=True)
        attn = jnp.dot(expo.astype(BF16), values, preferred_element_type=F32)
        attn = (attn * scale).astype(BF16)
        attn = jnp.concatenate([attn[i * rows : (i + 1) * rows] for i in range(heads)], axis=1)

        if t == 0:
            wo_copy.wait()

        def term(d):
            span = cols_of(flipped(me, d))
            return jnp.dot(attn, wo[:, span], preferred_element_type=F32)

        kept = cross if t < last else odd + [0]
        p_copies = {}
        for ks in (kept[:1], kept[1:]):
            for k in ks:
                e = k - 1 if k % 2 else k + 1
                sbuf[t, e] = term(e).astype(BF16)
            for k in ks:
                e = k - 1 if k % 2 else k + 1
                p_copies[k] = send(
                    sbuf.at[t, e],
                    pbuf.at[t, k],
                    p_send.at[t, k],
                    p_recv.at[t, k],
                    (section, partner),
                )
        if t == 0:
            pl.semaphore_wait(ready, 1)
        r_copies = {}
        for k in kept:
            if k == kept[0]:
                own_terms = {j: term(j) for j in kept[:2]}
            if k == kept[1]:
                own_terms.update({j: term(j) for j in kept[2:]})
            p_copies[k].wait_recv()
            pair = own_terms[k] + pbuf[t, k].astype(F32)
            if k == 0:
                total = pair
                continue
            sbuf[t, k] = pair.astype(BF16)
            target = nxt if t < last else section
            r_copies[k] = send(
                sbuf.at[t, k],
                rbuf.at[t, k],
                r_send.at[t, k],
                r_recv.at[t, k],
                (target, flipped(me, k)),
            )
        if t < last:
            send_cache(t + 1)
        if t == 0:
            own_cols = pltpu.make_async_copy(
                down_hbm.at[0, :, :, cols_of(me)], dparts.at[me], d_recv.at[0]
            )
            own_cols.start()
            own_cols.wait()
            for d in range(1, parts):
                d_copies[d].wait_recv()
            for p in range(parts):
                for a in range(adapters):
                    lo = a * rank_full + p * rank_share
                    dcols32[lo : lo + rank_share, :] = dparts[p, a].astype(F32)
            dcols[...] = dcols32[...].T.astype(BF16)
        late = [id(copy) for copy in r_copies.values()]
        for copy in pending:
            if id(copy) not in late:
                copy.wait_send()
        pending[:] = list(r_copies.values())
        if t < last:
            onehot_next = onehot_of(gidx_next)
            res_copies[t].wait_recv()
            total = res[t].astype(F32)
            for k in cross:
                r_copies[k].wait_recv()
                total += rbuf[t, k].astype(F32)
            result = total.astype(BF16)
            xbuf[t + 1, 0] = result
            x_copies = spread_x(t + 1, xbuf.at[t + 1, 0])
            h = (result.astype(F32) * gain[:, cols_of(me)].astype(F32)).astype(BF16)
            u_part = jnp.dot(h, dcols[...], preferred_element_type=F32)
            u_part = u_part * onehot_next
            u_own = u_part[:, :LANES]
            for i in range(1, full // LANES):
                u_own += u_part[:, i * LANES : (i + 1) * LANES]
            ubuf[t + 1, 0] = u_own.astype(BF16)
            u_copies = spread_u(t + 1)
            if t + 1 < last:
                res_copies[t + 1] = send_res(t + 1, xbuf.at[t + 1, 0])
            out_copies[t] = send(
                xbuf.at[t + 1, 0], out_ref.at[0, t], o_send.at[t], o_recv.at[t], (prv, me)
            )
        else:
            for k in near_odd:
                r_copies[k].wait_recv()
                total += rbuf[t, k].astype(F32)
            out_ref[0, t] = (xbuf[t, 0].astype(F32) + total).astype(BF16)

    for t in range(last):
        out_copies[t].wait_recv()
    for copy in pending:
        copy.wait_send()


def local(
    hidden_entering,
    layer_norm_gain,
    query_matrix,
    output_matrix,
    adapter_down_weight,
    adapter_up_weight,
    key_value_cache,
    adapter_index,
    cached_lengths,
):
    sections = lax.axis_size("section")
    parts = lax.axis_size("tp")
    rows, share = hidden_entering.shape[1:]
    ticks, _, context, _ = key_value_cache.shape[1:]
    width, feats = query_matrix.shape[1:]
    adapters, rank_share = adapter_down_weight.shape[1:3]
    rank_full = adapter_up_weight.shape[2]
    ranks, full = adapters * rank_share, adapters * rank_full
    vmem = pl.BlockSpec(memory_space=pltpu.VMEM)
    hbm = pl.BlockSpec(memory_space=pl.ANY)
    dma = pltpu.SemaphoreType.DMA
    blocks = pltpu.VMEM((ticks, parts, rows, share), BF16)
    return pl.pallas_call(
        functools.partial(kernel, sections, parts),
        out_shape=pltpu.VMEM((1, ticks, rows, share), BF16),
        in_specs=[hbm] * 9,
        out_specs=vmem,
        scratch_shapes=[
            pltpu.SemaphoreType.REGULAR,
            pltpu.SMEM(adapter_index.shape, jnp.int32),
            pltpu.SMEM(cached_lengths.shape, jnp.int32),
            dma((2,)),
            pltpu.VMEM((width, feats), BF16),
            pltpu.VMEM((feats, width), BF16),
            pltpu.VMEM((1, width), BF16),
            pltpu.VMEM((adapters, rank_full, feats), BF16),
            pltpu.VMEM((2, parts // 2, adapters, rank_share, share), BF16),
            pltpu.VMEM((parts // 2, 2 * ranks, share), F32),
            pltpu.VMEM((parts // 2, share, 2 * ranks), BF16),
            pltpu.VMEM((parts, adapters, rank_share, share), BF16),
            pltpu.VMEM((full, share), F32),
            pltpu.VMEM((share, full), BF16),
            pltpu.VMEM((ticks, rows, context, HD), BF16),
            pltpu.VMEM((ticks, rows, context, HD), BF16),
            blocks,
            pltpu.VMEM((ticks, parts, rows, LANES), BF16),
            pltpu.VMEM((ticks, rows, share), BF16),
            pltpu.VMEM((parts, rows, share), F32),
            blocks,
            blocks,
            blocks,
            dma((parts,)),
            dma(()),
            dma(()),
            dma(()),
            dma(()),
            dma((parts // 2,)),
            dma((2, parts // 2)),
            dma((parts,)),
            dma((parts,)),
            dma((ticks, 2, parts)),
            dma((ticks, 2, parts)),
            dma((ticks, parts)),
            dma((ticks, parts)),
            dma((ticks, parts)),
            dma((ticks, parts)),
            dma((ticks, parts)),
            dma((ticks, parts)),
            dma((ticks, parts)),
            dma((ticks, parts)),
            dma((ticks,)),
            dma((ticks,)),
            dma((ticks,)),
            dma((ticks,)),
        ],
        compiler_params=pltpu.CompilerParams(
            collective_id=0, has_side_effects=True, vmem_limit_bytes=56 << 20
        ),
    )(
        adapter_index,
        cached_lengths,
        hidden_entering,
        layer_norm_gain,
        query_matrix,
        output_matrix,
        adapter_down_weight,
        adapter_up_weight,
        key_value_cache,
    )


def solution(mesh):
    placed = (
        P("section", None, "tp"),
        P("section", None),
        P("section", None, "tp"),
        P("section", "tp", None),
        P("section", None, "tp", None),
        P("section", None, None, "tp"),
        P("section", None, "tp", None, None),
        P(),
        P(),
    )
    return jax.shard_map(
        local, mesh=mesh, in_specs=placed, out_specs=P("section", None, None, "tp"), check_vma=False
    )
```
